256 devices in a mesh: grp: 32 (over z, x), vocab: 8 (over y, core).
Axes of the slice: x: 4, y: 4, z: 8, core: 2. Of those that a mesh axis runs over, the one named last changes fastest.
Arguments:
- final_hidden: bfloat16 [8192, 2048], P('grp')
- norm_gain: float32 [2048], replicated, may hold values from 0.5 to 1.5
- head_weight: bfloat16 [50176, 2048], P(('vocab', 'grp'))
- token_ids: int32 [8192], replicated, may hold values from 0 to 50175
- group_lengths: int32 [32], replicated, may hold values from 1 to 256, as said below
- segment_ids: int32 [8192], P('grp'), may hold values from 0 to 3, as said below
- continues: int32 [32], replicated, may hold values from 0 to 1, as said below
- layer_input: bfloat16 [8192, 2048], P('grp')
- key_weight: bfloat16 [2048, 2048], P(None, 'vocab')
- key_gain: float32 [2048], P('vocab'), may hold values from 0.5 to 1.5
- positions: int32 [8192], P('grp'), may hold values from 0 to 16383
- key_rows: int32 [800], P('grp'), may hold values from 0 to 255, as said below
Outputs:
- token_logprob: float32 [8192], P('grp')
- token_entropy: float32 [8192], P('grp')
- request_mean: float32 [128], P('grp')
- keys: bfloat16 [800, 2048], P('grp', 'vocab')
The draws below stay inside these ranges and needn't reach their ends.
Inputs may be any that keep to these rules, and one draw needn't show every extreme that they name: For every g below 16, group_lengths[g] + group_lengths[g + 16] <= 320; groups 0 and 16 reach that bound, and group 0 fills all 256 slots. `segment_ids`: never falls along a group's slots. `continues`: 0 for odd g, 1 for g = 0 and for g = 30. `key_rows`: each entry is below its group's length.
All inputs are finite; a program needn't handle non-finite values.
Results may differ from the reference program's by a relative error of at most 0.0071.
Values may be sent and summed in bfloat16 or wider, within the bound.
A program may use at most 128 MiB of HBM per device.

```python
import math
import jax
import jax.numpy as jnp
import numpy as np
from jax import lax

D = 2048
HD = 128
CAP = 256
SEGS = 4
BAL = 160
KROWS = 25
KD = 2048
VOCAB = 50176
TOKENS = 8192
N_GRP = 32


def raw_rows(key, index):
    base = jax.random.fold_in(key, 11)

    def one_row(item):
        return jax.random.normal(jax.random.fold_in(base, item), (D,), jnp.float32)
    return jnp.clip(jax.vmap(one_row)(index), -5.0, 5.0)


def head_table(key, index):
    raw = raw_rows(key, index)
    factor = 1.0 + 0.08 * (index.astype(jnp.float32) / VOCAB - 0.5)
    return raw * 0.075 * factor[:, None]


def anchor_picks(key):
    anchors = jax.random.randint(jax.random.fold_in(key, 12), (8,), 0, VOCAB)
    partners = (anchors + VOCAB // 2) % VOCAB
    strength = jnp.array([0.9, 1.2, 1.8, 0.9, 1.2, 1.8, 1.2, 1.8], jnp.float32)
    return (anchors, partners, strength)


def length_table(key):
    groups = TOKENS // CAP
    half = groups // 2
    base = jax.random.fold_in(key, 21)
    total = jax.random.randint(jax.random.fold_in(base, 1), (half,), BAL, 2 * BAL + 1)
    total = total.at[0].set(2 * BAL)
    lowest = jnp.maximum(1, total - CAP)
    highest = jnp.minimum(CAP, total - 1)
    choose = jax.random.randint(jax.random.fold_in(base, 2), (half,), 0, 1 << 20)
    first = lowest + choose % (highest - lowest + 1)
    first = first.at[0].set(CAP)
    return jnp.concatenate([first, total - first]).astype(jnp.int32)


def scaled_field(key):
    base = jnp.clip(jax.random.normal(jax.random.fold_in(key, 1), (TOKENS, D), jnp.float32), -5.0, 5.0)
    row_scale = jnp.exp(jax.random.uniform(jax.random.fold_in(key, 2), (TOKENS, 1), jnp.float32, 0.0, jnp.log(10.0)))
    col_scale = jnp.exp(jax.random.uniform(jax.random.fold_in(key, 3), (1, D), jnp.float32, 0.0, jnp.log(10.0)))
    return base * row_scale * col_scale


def draw_head_weight(key, part):
    table = head_table(key, jnp.arange(VOCAB, dtype=jnp.int32))
    anchors, partners, strength = anchor_picks(key)
    anchor_rows = raw_rows(key, anchors) * (120.0 / D) * strength[:, None]
    noise = jax.random.normal(jax.random.fold_in(key, 13), (8, D), jnp.float32) * 0.075 * 0.12
    partner_rows = anchor_rows * (1.0 - 0.016 / strength[:, None]) + noise
    table = table.at[anchors].set(anchor_rows).at[partners].set(partner_rows)
    return table.astype(jnp.bfloat16)


def draw_final_hidden(key, part):
    field = scaled_field(jax.random.fold_in(key, 51))
    anchors, partners, strength = anchor_picks(key)
    aligned = raw_rows(key, anchors)
    rows = jnp.arange(8, dtype=jnp.int32) * (TOKENS // 8)
    field = field.at[rows].set(aligned)
    return field.astype(jnp.bfloat16)


def draw_layer_input(key, part):
    return scaled_field(jax.random.fold_in(key, 61)).astype(jnp.bfloat16)


def draw_key_weight(key, part):
    base = jnp.clip(jax.random.normal(jax.random.fold_in(key, 71), (D, KD), jnp.float32), -5.0, 5.0)
    columns = jnp.arange(KD).astype(jnp.float32)
    rising = jnp.exp(0.5 * jnp.log(3.0) * columns / KD)
    return (base * rising[None, :] / jnp.sqrt(jnp.float32(D))).astype(jnp.bfloat16)


def draw_group_lengths(key, part):
    return length_table(key)


def draw_segment_ids(key, part):
    lengths = length_table(key)
    groups = TOKENS // CAP
    raw = jax.random.randint(jax.random.fold_in(key, 31), (groups, SEGS - 1), 0, 1 << 20)
    span = jnp.maximum(lengths - 1, 1)
    breaks = 1 + raw % span[:, None]
    slots = jnp.arange(CAP, dtype=jnp.int32)
    labels = jnp.sum((breaks[:, None, :] <= slots[None, :, None]).astype(jnp.int32), axis=2)
    return labels.reshape(-1).astype(jnp.int32)


def draw_continues(key, part):
    groups = TOKENS // CAP
    raw = jax.random.randint(jax.random.fold_in(key, 41), (groups,), 0, 2)
    even = jnp.arange(groups, dtype=jnp.int32) % 2 == 0
    flags = jnp.where(even, raw, 0)
    return flags.at[0].set(1).at[groups - 2].set(1).astype(jnp.int32)


def draw_key_rows(key, part):
    lengths = length_table(key)
    groups = TOKENS // CAP
    raw = jax.random.randint(jax.random.fold_in(key, 81), (groups, KROWS), 0, 1 << 20)
    rows = raw % lengths[:, None]
    rows = rows.at[0, 0].set(CAP - 1).at[1, 0].set(0)
    return rows.reshape(-1).astype(jnp.int32)


def plant(values, own_key, smallest, top_value):
    place = [jax.random.randint(jax.random.fold_in(own_key, axis), (), 0, length) for axis, length in enumerate(values.shape)]
    widest = values.shape.index(max(values.shape))
    beside = place[:widest] + [(place[widest] + 1) % values.shape[widest]] + place[widest + 1:]
    return values.at[tuple(place)].set(smallest).at[tuple(beside)].set(top_value)


def rank_table(count, lean):
    loads = [(1 << 20) // math.isqrt(standing ** lean) + 1 for standing in range(1, count + 1)]
    scale = 1 + sum(loads) // (1 << 30)
    return np.cumsum(np.array([max(1, weight // scale) for weight in loads]))


def ranked_ids(own_key, shape, number_of, skew):
    grid = rank_table(number_of, skew)
    lot = jax.random.randint(jax.random.fold_in(own_key, 1), shape, 0, int(grid[number_of - 1]))
    grade = jnp.searchsorted(jnp.asarray(grid, jnp.int32), lot, side="right")
    return jax.random.permutation(jax.random.fold_in(own_key, 2), number_of)[grade].astype(jnp.int32)


def setup_inputs(seed: int = 0) -> dict:
    arg_keys = jax.random.split(jax.random.key(seed), 13)
    return {
        "final_hidden": draw_final_hidden(jax.random.fold_in(arg_keys[12], 71), 0),
        "norm_gain": jnp.clip(1.0 + 0.1 * jax.random.normal(arg_keys[1], (D,), jnp.float32), 0.5, 1.5),
        "head_weight": draw_head_weight(jax.random.fold_in(arg_keys[12], 71), 0),
        "token_ids": plant(ranked_ids(arg_keys[3], (TOKENS,), VOCAB, 2), jax.random.fold_in(arg_keys[3], 3), 0, VOCAB - 1).astype(jnp.int32),
        "group_lengths": draw_group_lengths(jax.random.fold_in(arg_keys[12], 71), 0),
        "segment_ids": draw_segment_ids(jax.random.fold_in(arg_keys[12], 71), 0),
        "continues": draw_continues(jax.random.fold_in(arg_keys[12], 71), 0),
        "layer_input": draw_layer_input(jax.random.fold_in(arg_keys[12], 71), 0),
        "key_weight": draw_key_weight(jax.random.fold_in(arg_keys[12], 71), 0),
        "key_gain": jnp.clip(1.0 + 0.1 * jax.random.normal(arg_keys[9], (KD,), jnp.float32), 0.5, 1.5),
        "positions": plant(jax.random.randint(arg_keys[10], (TOKENS,), 0, 16384), jax.random.fold_in(arg_keys[10], 1), 0, 16383).astype(jnp.int32),
        "key_rows": draw_key_rows(jax.random.fold_in(arg_keys[12], 71), 0),
    }


NORM_EPS = 1e-06
ROPE_BASE = 500000.0

def normalize(hidden, gain):
    widened = hidden.astype(jnp.float32)
    meansq = lax.optimization_barrier(jnp.mean(widened * widened, axis=-1, keepdims=True))
    return (widened * lax.rsqrt(meansq + NORM_EPS) * gain).astype(jnp.bfloat16)

def group_stats(normed_rows, targets, weight):
    product = jnp.dot(normed_rows, weight.T, preferred_element_type=jnp.float32)
    logits = lax.optimization_barrier(product.astype(jnp.bfloat16)).astype(jnp.float32)
    highest = lax.optimization_barrier(jnp.max(logits, axis=1))
    shifted = jnp.exp(logits - highest[:, None])
    expsum = lax.optimization_barrier(jnp.sum(shifted, axis=1))
    moment = lax.optimization_barrier(jnp.sum(shifted * logits, axis=1))
    picked = jnp.take_along_axis(logits, targets[:, None], axis=1)[:, 0]
    logsum = highest + jnp.log(expsum)
    return (picked - logsum, logsum - moment / expsum)

def rotate(values, places):
    count = values.shape[0]
    heads = values.shape[1] // HD
    half = HD // 2
    shaped = values.reshape(count, heads, HD)
    steps = jnp.arange(half).astype(jnp.float32)
    freqs = jnp.exp(-(2.0 * steps / HD) * jnp.log(jnp.float32(ROPE_BASE)))
    angles = places[:, None] * freqs[None, :]
    cosine = jnp.cos(angles)[:, None, :]
    sine = jnp.sin(angles)[:, None, :]
    first = shaped[..., :half]
    second = shaped[..., half:]
    turned = jnp.concatenate([first * cosine - second * sine, second * cosine + first * sine], axis=-1)
    return turned.reshape(count, heads * HD)

def reference(final_hidden, norm_gain, head_weight, token_ids, group_lengths, segment_ids, continues, layer_input, key_weight, key_gain, positions, key_rows):
    groups = N_GRP
    normed = normalize(final_hidden, norm_gain).reshape(groups, CAP, D)
    targets = token_ids.reshape(groups, CAP)
    logprob, entropy = lax.map(lambda pair: group_stats(pair[0], pair[1], head_weight), (normed, targets))
    slots = jnp.arange(CAP, dtype=jnp.int32)
    live = slots[None, :] < group_lengths[:, None]
    logprob = jnp.where(live, logprob, 0.0)
    entropy = jnp.where(live, entropy, 0.0)
    segs = segment_ids.reshape(groups, CAP)
    labels = jnp.arange(SEGS, dtype=jnp.int32)
    member = (segs[:, :, None] == labels[None, None, :]) & live[:, :, None]
    sums = lax.optimization_barrier(jnp.sum(jnp.where(member, logprob[:, :, None], 0.0), axis=1))
    counts = lax.optimization_barrier(jnp.sum(member.astype(jnp.float32), axis=1))
    group_index = jnp.arange(groups, dtype=jnp.int32)
    partner = jnp.bitwise_xor(group_index, 1)
    partner_sums = sums[partner]
    partner_counts = counts[partner]
    is_even = group_index % 2 == 0
    joined = jnp.where(is_even, continues, continues[partner]) == 1
    my_last = jnp.take_along_axis(segs, (group_lengths - 1)[:, None].astype(jnp.int32), axis=1)[:, 0]
    partner_last = lax.optimization_barrier(jnp.max(jnp.where(partner_counts > 0, labels[None, :], 0), axis=1))
    extra_sum = jnp.where(is_even, partner_sums[:, 0], jnp.take_along_axis(partner_sums, partner_last[:, None], axis=1)[:, 0])
    extra_count = jnp.where(is_even, partner_counts[:, 0], jnp.take_along_axis(partner_counts, partner_last[:, None], axis=1)[:, 0])
    target_slot = jnp.where(is_even, my_last, 0)
    update = joined[:, None] & (labels[None, :] == target_slot[:, None])
    total_sum = sums + jnp.where(update, extra_sum[:, None], 0.0)
    total_count = counts + jnp.where(update, extra_count[:, None], 0.0)
    request_mean = total_sum / jnp.maximum(total_count, 1.0)
    row_index = jnp.arange(groups * KROWS, dtype=jnp.int32) // KROWS * CAP + key_rows
    chosen = jnp.take(layer_input, row_index, axis=0)
    projected = jnp.dot(chosen, key_weight, preferred_element_type=jnp.float32)
    scale = jnp.sqrt(lax.optimization_barrier(jnp.mean(projected * projected, axis=1)) + NORM_EPS)
    normal_keys = projected / scale[:, None] * key_gain
    places = jnp.take(positions, row_index).astype(jnp.float32)
    keys = rotate(normal_keys, places).astype(jnp.bfloat16)
    return (logprob.reshape(-1), entropy.reshape(-1), request_mean.reshape(-1), keys)
```

```python
import jax
import jax.numpy as jnp
import numpy as np
from jax import lax
from jax.experimental import pallas as pl
from jax.experimental.pallas import tpu as pltpu
from jax.sharding import PartitionSpec as P

HD = 128
SEGS = 4
NORM_EPS = 1e-06
ROPE_BASE = 500000.0

NX, NY, NZ = 4, 4, 8
ROWS = 128
BOTH = 256
DIM = 2048
WROWS = 196
WHALF = DIM // 2
ACOLS = 512
SCOLS = (DIM - ACOLS) // NY
KROWS = 25
KPAD = 32
MESH = pl.DeviceIdType.MESH

TWO_PI_1 = 6.28125
TWO_PI_2 = float(np.float32(round((2 * np.pi - TWO_PI_1) * 2**20) / 2**20))
TWO_PI_3 = float(2 * np.pi - TWO_PI_1 - TWO_PI_2)


def place_of(d):
    return {0: (0, 0), 4: (0, 1), 1: (1, 0), 7: (1, 1), 2: (2, 0), 6: (2, 1), 3: (3, 0), 5: (3, 1)}[d]


def merged(maxes, sums, moments, picks):
    top = jnp.max(maxes, axis=0, keepdims=True)
    scale = jnp.exp(maxes - top)
    return (
        top,
        jnp.sum(sums * scale, axis=0, keepdims=True),
        jnp.sum(moments * scale, axis=0, keepdims=True),
        jnp.sum(picks, axis=0, keepdims=True),
    )


def kernel(
    hidden, weight, layer_input, key_weight,
    gain, tokens, lengths, segments, continues, key_gain, positions, key_rows, freqs,
    logprob_out, entropy_out, mean_out, keys_out,
    raw, held, wts, lin, kwt, toks, acc, gathered, part, parts,
    squares, all_squares, pair_own, pair_got,
    local_sems, send_sems, recv_sems,
):
    grp = lax.axis_index("grp")
    voc = lax.axis_index("vocab")
    x, z = lax.rem(grp, NX), lax.div(grp, NX)
    y, c = lax.div(voc, 2), lax.rem(voc, 2)

    def device(xx, yy, zz, cc):
        return (zz * NX + xx, yy * 2 + cc)

    def up(d):
        return device(x, y, lax.rem(z + d, NZ), c)

    x_up = device(lax.rem(x + 1, NX), y, z, c)
    x_down = device(lax.rem(x + NX - 1, NX), y, z, c)
    y_up = device(x, lax.rem(y + 1, NY), z, c)
    y_down = device(x, lax.rem(y + NY - 1, NY), z, c)
    sibling = device(x, y, z, 1 - c)
    partner = device(x + 1 - 2 * lax.rem(x, 2), y, z, c)
    voc_peers = [(grp, lax.rem(voc + d, 8)) for d in range(1, 8)]

    ids = {}

    def remote(name, src, dst, to):
        number = ids.setdefault(name, len(ids))
        return pltpu.make_async_remote_copy(
            src_ref=src, dst_ref=dst, send_sem=send_sems.at[number], recv_sem=recv_sems.at[number],
            device_id=to, device_id_type=MESH,
        )

    sent = []

    def send(name, src, dst, to):
        copy = remote(name, src, dst, to)
        copy.start()
        sent.append(copy)

    def receive(name, dst, to):
        remote(name, dst, dst, to).wait_recv()

    local_copies = [
        pltpu.make_async_copy(hidden.at[pl.ds(pl.multiple_of(c * ROWS, ROWS), ROWS)], raw, local_sems.at[0]),
        pltpu.make_async_copy(weight, wts.at[0], local_sems.at[1]),
        pltpu.make_async_copy(layer_input, lin, local_sems.at[2]),
        pltpu.make_async_copy(key_weight, kwt, local_sems.at[3]),
    ]
    for copy in local_copies:
        copy.start()

    barrier = pltpu.get_barrier_semaphore()
    peers = [up(d) for d in range(1, NZ)] + voc_peers + [x_up, x_down]
    for peer in peers:
        pl.semaphore_signal(barrier, inc=1, device_id=peer, device_id_type=MESH)
    pl.semaphore_wait(barrier, len(peers))

    left, right = pl.ds(0, WHALF), pl.ds(WHALF, WHALF)
    send("w+L", weight.at[:, left], wts.at[1, :, left], x_up)
    send("w-R", weight.at[:, right], wts.at[2, :, right], x_down)
    send("w+R", weight.at[:, right], wts.at[1, :, right], x_up)
    send("w-L", weight.at[:, left], wts.at[2, :, left], x_down)
    send("w0", weight, wts.at[4], sibling)

    def to_sibling(slot, cols, name):
        send("s" + name, wts.at[slot, :, cols], wts.at[4 + slot, :, cols], sibling)

    def from_sibling(slot, cols, name):
        receive("s" + name, wts.at[4 + slot, :, cols], sibling)

    local_copies[0].wait()
    total = jnp.zeros((ROWS, HD), jnp.float32)
    for j in range(DIM // HD):
        block = raw[:, j * HD:(j + 1) * HD].astype(jnp.float32)
        total = total + block * block
    inverse = lax.rsqrt(jnp.sum(total, axis=1, keepdims=True) / DIM + NORM_EPS)
    for j in range(DIM // HD):
        block = raw[:, j * HD:(j + 1) * HD].astype(jnp.float32)
        held[0, 0:ROWS, j * HD:(j + 1) * HD] = (block * inverse * gain[j:j + 1, :]).astype(jnp.bfloat16)

    def rows_of(d, cols, first=0, count=ROWS):
        pair, half = place_of(d)
        return held.at[pair, pl.ds(half * ROWS + first, count), cols]

    def share(yy):
        return pl.ds(pl.multiple_of(ACOLS + SCOLS * lax.rem(yy, NY), HD), SCOLS)

    alone = pl.ds(0, ACOLS)
    LAST = {("S", "+"): 3, ("S", "-"): 4, ("A", "+"): 4, ("A", "-"): 3}

    def away(way, k):
        return (NZ - k) % NZ if way == "+" else k

    def z_send(kind, way, k):
        cols = alone if kind == "A" else share(y)
        send(
            f"z{kind}{way}{k}", rows_of(away(way, k - 1), cols), rows_of(away(way, k), cols),
            up(1) if way == "+" else up(NZ - 1),
        )

    def z_receive(kind, k):
        for way in "+-":
            if k > LAST[kind, way]:
                continue
            d = away(way, k)
            cols = alone if kind == "A" else share(y)
            receive(f"z{kind}{way}{k}", rows_of(d, cols), up(1))
            if k < LAST[kind, way]:
                z_send(kind, way, k + 1)
            if kind == "S":
                send(f"y+{d}", rows_of(d, cols), rows_of(d, cols), y_up)
                send(f"y-{d}", rows_of(d, cols), rows_of(d, cols), y_down)

    def groups_at(k):
        return sorted({away("+", k), away("-", k)})

    half_rows = ROWS // 2

    def y_receive(k):
        for d in groups_at(k):
            below, above = share(y + NY - 1), share(y + 1)
            receive(f"y+{d}", rows_of(d, below), y_up)
            ref = rows_of(d, below, 0, half_rows)
            send(f"yf+{d}", ref, ref, y_up)
            receive(f"y-{d}", rows_of(d, above), y_down)
            ref = rows_of(d, above, half_rows, half_rows)
            send(f"yf-{d}", ref, ref, y_down)

    def y_finish(k):
        for d in groups_at(k):
            across = share(y + 2)
            receive(f"yf+{d}", rows_of(d, across, 0, half_rows), y_up)
            receive(f"yf-{d}", rows_of(d, across, half_rows, half_rows), y_down)

    for kind in "SA":
        for way in "+-":
            z_send(kind, way, 1)

    row_ids = lax.broadcasted_iota(jnp.int32, (KPAD, BOTH), 0)
    col_ids = lax.broadcasted_iota(jnp.int32, (KPAD, BOTH), 1)
    wanted = jnp.zeros((KPAD, BOTH), jnp.int32)
    for i in range(KROWS):
        wanted = jnp.where(row_ids == i, key_rows[i], wanted)
    picks = jnp.where(col_ids == wanted, 1.0, 0.0)
    local_copies[2].wait()
    local_copies[3].wait()
    chosen = jnp.dot(picks.astype(jnp.bfloat16), lin[...], preferred_element_type=jnp.float32)
    projected = jnp.dot(chosen.astype(jnp.bfloat16), kwt[...], preferred_element_type=jnp.float32)
    squares[...] = jnp.broadcast_to(jnp.sum(projected * projected, axis=1, keepdims=True), (KPAD, HD))
    for i, peer in enumerate(voc_peers):
        send(f"k{i + 1}", squares, all_squares.at[i + 1], peer)

    for p in range(4):
        acc[p, 0:1, :] = jnp.full((1, BOTH), -jnp.inf, jnp.float32)
        acc[p, 1:8, :] = jnp.zeros((7, BOTH), jnp.float32)
        for half, d in enumerate([d for d in (0, 4, 1, 7, 2, 6, 3, 5) if place_of(d)[0] == p]):
            row = (lax.rem(z + d, NZ) * NX + x) * 2 + c
            toks[p, 0:1, half * ROWS:(half + 1) * ROWS] = tokens[pl.ds(row, 1), :]

    def chunk(p, w):
        other, turn = lax.div(w, 4), lax.rem(w, 4)
        shift = jnp.where(turn == 0, 0, jnp.where(turn == 1, 3, jnp.where(turn == 2, 1, 2)))
        first = (y * 2 + lax.rem(c + other, 2)) * (WROWS * NX * NZ) + (z * NX + lax.rem(x + shift, NX)) * WROWS
        logits = lax.dot_general(
            wts[w], held[p], (((1,), (1,)), ((), ())), preferred_element_type=jnp.float32
        ).astype(jnp.bfloat16).astype(jnp.float32)
        old = acc[p, 0:1, :]
        top = jnp.maximum(old, jnp.max(logits, axis=0, keepdims=True))
        shifted = jnp.exp(logits - top)
        scale = jnp.exp(old - top)
        hit = lax.broadcasted_iota(jnp.int32, (WROWS, BOTH), 0) == toks[p, 0:1, :] - first
        acc[p, 0:1, :] = top
        acc[p, 1:2, :] = acc[p, 1:2, :] * scale + jnp.sum(shifted, axis=0, keepdims=True)
        acc[p, 2:3, :] = acc[p, 2:3, :] * scale + jnp.sum(shifted * logits, axis=0, keepdims=True)
        acc[p, 3:4, :] = acc[p, 3:4, :] + jnp.sum(jnp.where(hit, logits, 0.0), axis=0, keepdims=True)

    def run(start, pairs, blocks, slot_of):
        def step(i, carry):
            chunk(start + lax.div(i, blocks), slot_of(lax.rem(i, blocks)))
            return carry
        lax.fori_loop(0, pairs * blocks, step, 0)

    def own_slots(i):
        return 4 * i

    def near_slots(i):
        return 1 + lax.rem(i, 2) + 4 * lax.div(i, 2)

    def most_slots(i):
        return i + lax.div(i, 3)

    def far_slots(i):
        return 3 + 4 * i

    z_receive("S", 1)
    z_receive("A", 1)

    for i in range(7):
        receive(f"k{i + 1}", all_squares.at[i + 1], sibling)
    square_sum = squares[...]
    for i in range(7):
        square_sum = square_sum + all_squares[i + 1]
    spread = jnp.sqrt(square_sum / (HD * 16) + NORM_EPS)
    places_row = jnp.concatenate([positions[0:1, :], positions[1:2, :]], axis=1).astype(jnp.float32)
    places = jnp.sum(picks * places_row, axis=1, keepdims=True)
    angles = places * freqs[0:1, :]
    turns = jnp.floor(angles * (0.5 / np.pi) + 0.5)
    angles = ((angles - turns * TWO_PI_1) - turns * TWO_PI_2) - turns * TWO_PI_3
    lanes = lax.broadcasted_iota(jnp.int32, (KPAD, HD), 1)
    cosine = jnp.cos(angles)
    sine = jnp.sin(angles)
    sine = jnp.where(lanes < HD // 2, -sine, sine)
    for head in range(2):
        values = projected[:, head * HD:(head + 1) * HD] / spread * key_gain[head:head + 1, :]
        turned = values * cosine + pltpu.roll(values, HD // 2, 1) * sine
        keys_out[:, head * HD:(head + 1) * HD] = turned[0:KROWS].astype(jnp.bfloat16)

    def weights_first():
        receive("w+L", wts.at[1, :, left], x_up)
        send("wf+", wts.at[1, :, left], wts.at[3, :, left], x_up)
        receive("w-R", wts.at[2, :, right], x_down)
        send("wf-", wts.at[2, :, right], wts.at[3, :, right], x_down)
        to_sibling(1, left, "+L")
        to_sibling(2, right, "-R")

    def weights_second():
        receive("w+R", wts.at[1, :, right], x_up)
        to_sibling(1, right, "+R")
        receive("w-L", wts.at[2, :, left], x_down)
        to_sibling(2, left, "-L")

    def weights_third():
        receive("wf+", wts.at[3, :, left], x_up)
        to_sibling(3, left, "f+")
        receive("wf-", wts.at[3, :, right], x_down)
        to_sibling(3, right, "f-")

    weights_first()
    y_receive(1)
    z_receive("S", 2)
    z_receive("A", 2)
    y_finish(1)
    local_copies[1].wait()
    receive("w0", wts.at[4], sibling)
    run(1, 1, 2, own_slots)
    y_receive(2)
    z_receive("S", 3)
    z_receive("A", 3)
    y_finish(2)
    run(2, 1, 2, own_slots)
    weights_second()
    y_receive(3)
    z_receive("S", 4)
    z_receive("A", 4)
    from_sibling(1, left, "+L")
    from_sibling(1, right, "+R")
    from_sibling(2, right, "-R")
    from_sibling(2, left, "-L")
    run(1, 2, 4, near_slots)
    y_finish(3)
    run(3, 1, 6, most_slots)
    y_receive(4)
    weights_third()
    y_finish(4)
    run(0, 1, 6, most_slots)
    from_sibling(3, left, "f+")
    from_sibling(3, right, "f-")
    run(0, 4, 2, far_slots)

    for d in range(1, NZ):
        pair, half = place_of(d)
        send(f"a{d}", acc.at[pair, :, pl.ds(half * ROWS, ROWS)], gathered.at[NZ - d], up(d))
    gathered[0] = acc[0, :, 0:ROWS]
    for d in range(1, NZ):
        receive(f"a{d}", gathered.at[NZ - d], up(d))
    stats = merged(*(gathered[:, i, :] for i in range(4)))
    for i in range(4):
        part[i:i + 1, :] = stats[i]
    part[4:8, :] = jnp.zeros((4, ROWS), jnp.float32)
    mine = c * NY + y
    for i, peer in enumerate(voc_peers):
        send(f"v{i + 1}", part, parts.at[mine], peer)
    parts[mine] = part[...]
    for i in range(7):
        source = lax.rem(voc + 7 - i, 8)
        receive(f"v{i + 1}", parts.at[lax.rem(source, 2) * NY + lax.div(source, 2)], sibling)

    lane = lax.broadcasted_iota(jnp.int32, (1, ROWS), 1)
    length = lengths[grp]
    sum_vec = jnp.zeros((1, ROWS), jnp.float32)
    count_vec = jnp.zeros((1, ROWS), jnp.float32)
    last = jnp.zeros((1, 1), jnp.float32)
    for half in range(2):
        top, expsum, moment, picked = merged(*(parts[half * NY:(half + 1) * NY, i, :] for i in range(4)))
        logsum = top + jnp.log(expsum)
        slot = lane + half * ROWS
        live = slot < length
        logprob = jnp.where(live, picked - logsum, 0.0)
        logprob_out[half:half + 1, :] = logprob
        entropy_out[half:half + 1, :] = jnp.where(live, logsum - moment / expsum, 0.0)
        label = segments[half:half + 1, :]
        last = last + jnp.sum(
            jnp.where(slot == length - 1, label.astype(jnp.float32), 0.0), axis=1, keepdims=True
        )
        for s in range(SEGS):
            member = live & (label == s)
            here = jnp.sum(jnp.where(member, logprob, 0.0), axis=1, keepdims=True)
            count = jnp.sum(jnp.where(member, 1.0, 0.0), axis=1, keepdims=True)
            sum_vec = sum_vec + jnp.where(lane == s, here, 0.0)
            count_vec = count_vec + jnp.where(lane == s, count, 0.0)
    pair_own[0:1, :] = sum_vec
    pair_own[1:2, :] = count_vec
    pair_own[2:8, :] = jnp.zeros((6, ROWS), jnp.float32)
    send("p", pair_own, pair_got, partner)
    receive("p", pair_got, partner)
    got_sums = pair_got[0:1, :]
    got_counts = pair_got[1:2, :]
    even = lax.rem(x, 2) == 0
    joined = continues[grp - lax.rem(grp, 2)] == 1
    lane_f = lane.astype(jnp.float32)
    got_last = jnp.max(jnp.where((got_counts > 0) & (lane < SEGS), lane_f, 0.0), axis=1, keepdims=True)
    source = jnp.where(even, 0.0, got_last)
    target = jnp.where(even, last, 0.0)
    extra_sum = jnp.sum(jnp.where(lane_f == source, got_sums, 0.0), axis=1, keepdims=True)
    extra_count = jnp.sum(jnp.where(lane_f == source, got_counts, 0.0), axis=1, keepdims=True)
    update = joined & (lane_f == target)
    total_sum = sum_vec + jnp.where(update, extra_sum, 0.0)
    total_count = count_vec + jnp.where(update, extra_count, 0.0)
    mean_out[...] = (total_sum / jnp.maximum(total_count, 1.0))[:, 0:SEGS]
    for copy in sent:
        copy.wait_send()


MESSAGES = 96


def local(
    final_hidden, norm_gain, head_weight, token_ids, group_lengths, segment_ids, continues,
    layer_input, key_weight, key_gain, positions, key_rows,
):
    steps = np.arange(HD // 2, dtype=np.float64)
    freqs = np.exp(-(2.0 * steps / HD) * np.log(ROPE_BASE)).astype(np.float32)
    freqs = jnp.asarray(np.concatenate([freqs, freqs])[None, :])
    anywhere = pl.BlockSpec(memory_space=pl.ANY)
    vmem = pl.BlockSpec(memory_space=pltpu.VMEM)
    smem = pl.BlockSpec(memory_space=pltpu.SMEM)
    f32, bf16 = jnp.float32, jnp.bfloat16
    logprob, entropy, mean, keys = pl.pallas_call(
        kernel,
        out_shape=(
            jax.ShapeDtypeStruct((2, ROWS), f32),
            jax.ShapeDtypeStruct((2, ROWS), f32),
            jax.ShapeDtypeStruct((1, SEGS), f32),
            jax.ShapeDtypeStruct((KROWS, BOTH), bf16),
        ),
        in_specs=[anywhere] * 4 + [vmem, vmem, smem, vmem, smem, vmem, vmem, smem, vmem],
        out_specs=(vmem,) * 4,
        scratch_shapes=[
            pltpu.VMEM((ROWS, DIM), bf16),
            pltpu.VMEM((4, BOTH, DIM), bf16),
            pltpu.VMEM((8, WROWS, DIM), bf16),
            pltpu.VMEM((2 * ROWS, DIM), bf16),
            pltpu.VMEM((DIM, BOTH), bf16),
            pltpu.VMEM((4, 1, BOTH), jnp.int32),
            pltpu.VMEM((4, 8, BOTH), f32),
            pltpu.VMEM((8, 8, ROWS), f32),
            pltpu.VMEM((8, ROWS), f32),
            pltpu.VMEM((8, 8, ROWS), f32),
            pltpu.VMEM((KPAD, HD), f32),
            pltpu.VMEM((8, KPAD, HD), f32),
            pltpu.VMEM((8, ROWS), f32),
            pltpu.VMEM((8, ROWS), f32),
            pltpu.SemaphoreType.DMA((4,)),
            pltpu.SemaphoreType.DMA((MESSAGES,)),
            pltpu.SemaphoreType.DMA((MESSAGES,)),
        ],
        compiler_params=pltpu.CompilerParams(
            collective_id=0, has_side_effects=True, vmem_limit_bytes=40 * 2**20
        ),
    )(
        final_hidden, head_weight, layer_input, key_weight,
        norm_gain.reshape(DIM // HD, HD), token_ids.reshape(-1, ROWS), group_lengths,
        segment_ids.reshape(2, ROWS), continues, key_gain.reshape(2, HD),
        positions.reshape(2, ROWS), key_rows, freqs,
    )
    return (logprob.reshape(-1), entropy.reshape(-1), mean.reshape(-1), keys)


def solution(mesh):
    in_specs = (
        P("grp", None),
        P(),
        P(("vocab", "grp"), None),
        P(),
        P(),
        P("grp"),
        P(),
        P("grp", None),
        P(None, "vocab"),
        P("vocab"),
        P("grp"),
        P("grp"),
    )
    out_specs = (P("grp"), P("grp"), P("grp"), P("grp", "vocab"))
    return jax.shard_map(local, mesh=mesh, in_specs=in_specs, out_specs=out_specs, check_vma=False)
```

```python
import jax
import jax.numpy as jnp
import numpy as np
from jax import lax
from jax.experimental import pallas as pl
from jax.experimental.pallas import tpu as pltpu
from jax.sharding import PartitionSpec as P

HD = 128
SEGS = 4
NORM_EPS = 1e-06
ROPE_BASE = 500000.0

NX, NY, NZ = 4, 4, 8
ROWS = 128
BOTH = 256
DIM = 2048
WROWS = 196
WPIECE = DIM // 4
SHARE = 352
ALONE = DIM - SHARE * NY
KROWS = 25
KPAD = 32
MESH = pl.DeviceIdType.MESH

TWO_PI_1 = 6.28125
TWO_PI_2 = float(np.float32(round((2 * np.pi - TWO_PI_1) * 2**20) / 2**20))
TWO_PI_3 = float(2 * np.pi - TWO_PI_1 - TWO_PI_2)


def place_of(d):
    return (0, 4, 1, 7, 2, 6, 3, 5).index(d)


def merged(maxes, sums, moments, picks):
    top = jnp.max(maxes, axis=0, keepdims=True)
    scale = jnp.exp(maxes - top)
    return (
        top,
        jnp.sum(sums * scale, axis=0, keepdims=True),
        jnp.sum(moments * scale, axis=0, keepdims=True),
        jnp.sum(picks, axis=0, keepdims=True),
    )


def kernel(
    hidden, weight, layer_input, key_weight,
    gain, tokens, lengths, segments, continues, key_gain, positions, key_rows, freqs,
    logprob_out, entropy_out, mean_out, keys_out,
    raw, held, wts, lin, kwt, toks, acc, gathered, part, parts,
    squares, all_squares, partner_segments,
    local_sems, send_sems, recv_sems,
):
    grp = lax.axis_index("grp")
    voc = lax.axis_index("vocab")
    x, z = lax.rem(grp, NX), lax.div(grp, NX)
    y, c = lax.div(voc, 2), lax.rem(voc, 2)

    def device(xx, yy, zz, cc):
        return (zz * NX + xx, yy * 2 + cc)

    def up(d):
        return device(x, y, lax.rem(z + d, NZ), c)

    x_up = device(lax.rem(x + 1, NX), y, z, c)
    x_down = device(lax.rem(x + NX - 1, NX), y, z, c)
    y_up = device(x, lax.rem(y + 1, NY), z, c)
    y_down = device(x, lax.rem(y + NY - 1, NY), z, c)
    sibling = device(x, y, z, 1 - c)
    partner = grp + 1 - 2 * lax.rem(x, 2)
    voc_peers = [(grp, lax.rem(voc + d, 8)) for d in range(1, 8)]

    ids = {}

    def remote(name, src, dst, to):
        number = ids.setdefault(name, len(ids))
        return pltpu.make_async_remote_copy(
            src_ref=src, dst_ref=dst, send_sem=send_sems.at[number], recv_sem=recv_sems.at[number],
            device_id=to, device_id_type=MESH,
        )

    sent = []

    def send(name, src, dst, to):
        copy = remote(name, src, dst, to)
        copy.start()
        sent.append(copy)

    def receive(name, dst, to):
        remote(name, dst, dst, to).wait_recv()

    local_copies = [
        pltpu.make_async_copy(hidden.at[pl.ds(pl.multiple_of(c * ROWS, ROWS), ROWS)], raw, local_sems.at[0]),
        pltpu.make_async_copy(weight, wts.at[0], local_sems.at[1]),
        pltpu.make_async_copy(layer_input, lin, local_sems.at[2]),
        pltpu.make_async_copy(key_weight, kwt, local_sems.at[3]),
    ]
    for copy in local_copies:
        copy.start()

    barrier = pltpu.get_barrier_semaphore()
    partners = [(partner, lax.rem(voc + d, 8)) for d in range(8)]
    other_x = device(lax.rem(x + 3 + 2 * lax.rem(x, 2), NX), y, z, c)
    peers = [up(d) for d in range(1, NZ)] + voc_peers + partners + [other_x]
    for peer in peers:
        pl.semaphore_signal(barrier, inc=1, device_id=peer, device_id_type=MESH)
    pl.semaphore_wait(barrier, len(peers))

    def piece(q):
        return pl.ds(q * WPIECE, WPIECE)

    def own_piece(way, first, count):
        cols = pl.ds(first * WPIECE, count * WPIECE)
        slot, to = (1, x_up) if way == "+" else (2, x_down)
        send(f"w{way}{first}", weight.at[:, cols], wts.at[slot, :, cols], to)

    own_piece("+", 0, 1)
    own_piece("-", 2, 1)

    def to_sibling(slot, first, count):
        cols = pl.ds(first * WPIECE, count * WPIECE)
        send(f"s{slot}{first}", wts.at[slot, :, cols], wts.at[4 + slot, :, cols], sibling)

    def from_sibling(slot, first, count):
        cols = pl.ds(first * WPIECE, count * WPIECE)
        receive(f"s{slot}{first}", wts.at[4 + slot, :, cols], sibling)

    def weights_near(i):
        receive(f"w+{i}", wts.at[1, :, piece(i)], x_up)
        send(f"wf+{i}", wts.at[1, :, piece(i)], wts.at[3, :, piece(i)], x_up)
        receive(f"w-{i + 2}", wts.at[2, :, piece(i + 2)], x_down)
        send(f"wf-{i + 2}", wts.at[2, :, piece(i + 2)], wts.at[3, :, piece(i + 2)], x_down)
        if i == 1:
            to_sibling(1, 0, 2)
            to_sibling(2, 2, 2)

    def weights_rest():
        cols = pl.ds(2 * WPIECE, 2 * WPIECE)
        receive("w+2", wts.at[1, :, cols], x_up)
        to_sibling(1, 2, 2)
        cols = pl.ds(0, 2 * WPIECE)
        receive("w-0", wts.at[2, :, cols], x_down)
        to_sibling(2, 0, 2)

    def weights_far(i):
        receive(f"wf+{i}", wts.at[3, :, piece(i)], x_up)
        to_sibling(3, i, 1)
        receive(f"wf-{i + 2}", wts.at[3, :, piece(i + 2)], x_down)
        to_sibling(3, i + 2, 1)

    local_copies[0].wait()
    total = jnp.zeros((ROWS, HD), jnp.float32)
    for j in range(DIM // HD):
        block = raw[:, j * HD:(j + 1) * HD].astype(jnp.float32)
        total = total + block * block
    inverse = lax.rsqrt(jnp.sum(total, axis=1, keepdims=True) / DIM + NORM_EPS)
    for j in range(DIM // HD):
        block = raw[:, j * HD:(j + 1) * HD].astype(jnp.float32)
        held[0, j * HD:(j + 1) * HD, :] = (block * inverse * gain[j:j + 1, :]).T.astype(jnp.bfloat16)

    def features(d, first, count):
        return held.at[place_of(d), pl.ds(first, count), :]

    def share(yy, first=0):
        return pl.multiple_of(ALONE + SHARE * lax.rem(yy, NY) + first, 16)

    LAST = {("S", "+"): 3, ("S", "-"): 4, ("A", "+"): 4, ("A", "-"): 3}

    def away(way, k):
        return (NZ - k) % NZ if way == "+" else k

    def z_part(kind, d):
        return features(d, 0, ALONE) if kind == "A" else features(d, share(y), SHARE)

    def z_send(kind, way, k):
        send(
            f"z{kind}{way}{k}", z_part(kind, away(way, k - 1)), z_part(kind, away(way, k)),
            up(1) if way == "+" else up(NZ - 1),
        )

    def z_receive(kind, k):
        for way in "+-":
            if k > LAST[kind, way]:
                continue
            d = away(way, k)
            receive(f"z{kind}{way}{k}", z_part(kind, d), up(1))
            if k < LAST[kind, way]:
                z_send(kind, way, k + 1)
        if kind == "S":
            ref = shares(k, share(y), SHARE)
            send(f"y+{k}", ref, ref, y_up)
            send(f"y-{k}", ref, ref, y_down)

    def shares(k, first, count):
        slots = pl.ds(2 * k, 2) if k < 4 else pl.ds(1, 1)
        return held.at[slots, pl.ds(first, count), :]

    half_share = SHARE // 2

    def y_receive(k):
        below, above = y + NY - 1, y + 1
        receive(f"y+{k}", shares(k, share(below), SHARE), y_up)
        ref = shares(k, share(below), half_share)
        send(f"yf+{k}", ref, ref, y_up)
        receive(f"y-{k}", shares(k, share(above), SHARE), y_down)
        ref = shares(k, share(above, half_share), half_share)
        send(f"yf-{k}", ref, ref, y_down)

    def y_finish(k):
        receive(f"yf+{k}", shares(k, share(y + 2), half_share), y_up)
        receive(f"yf-{k}", shares(k, share(y + 2, half_share), half_share), y_down)

    for kind in "SA":
        for way in "+-":
            z_send(kind, way, 1)
    own_piece("+", 1, 1)
    own_piece("-", 3, 1)
    own_piece("+", 2, 2)
    own_piece("-", 0, 2)
    send("w0", weight, wts.at[4], sibling)
    send("g", segments, partner_segments, partners[0])

    row_ids = lax.broadcasted_iota(jnp.int32, (KPAD, BOTH), 0)
    col_ids = lax.broadcasted_iota(jnp.int32, (KPAD, BOTH), 1)
    wanted = jnp.zeros((KPAD, BOTH), jnp.int32)
    for i in range(KROWS):
        wanted = jnp.where(row_ids == i, key_rows[i], wanted)
    picks = jnp.where(col_ids == wanted, 1.0, 0.0)
    local_copies[2].wait()
    local_copies[3].wait()
    chosen = jnp.dot(picks.astype(jnp.bfloat16), lin[...], preferred_element_type=jnp.float32)
    projected = jnp.dot(chosen.astype(jnp.bfloat16), kwt[...], preferred_element_type=jnp.float32)
    squares[...] = jnp.broadcast_to(jnp.sum(projected * projected, axis=1, keepdims=True), (KPAD, HD))
    for i, peer in enumerate(voc_peers):
        send(f"k{i + 1}", squares, all_squares.at[i + 1], peer)

    for p in range(4):
        acc[p, 0:1, :] = jnp.full((1, BOTH), -jnp.inf, jnp.float32)
        acc[p, 1:8, :] = jnp.zeros((7, BOTH), jnp.float32)
        for half, d in enumerate((0, 4, 1, 7, 2, 6, 3, 5)[2 * p:2 * p + 2]):
            row = (lax.rem(z + d, NZ) * NX + x) * 2 + c
            toks[p, 0:1, half * ROWS:(half + 1) * ROWS] = tokens[pl.ds(row, 1), :]

    def chunk(p, w):
        other, turn = divmod(w, 4)
        shift = (0, NX - 1, 1, 2)[turn]
        first = (y * 2 + lax.rem(c + other, 2)) * (WROWS * NX * NZ) + (z * NX + lax.rem(x + shift, NX)) * WROWS
        logits = lax.dot_general(
            wts[w], jnp.concatenate([held[2 * p], held[2 * p + 1]], axis=1),
            (((1,), (0,)), ((), ())), preferred_element_type=jnp.float32
        ).astype(jnp.bfloat16).astype(jnp.float32)
        old = acc[p, 0:1, :]
        top = jnp.maximum(old, jnp.max(logits, axis=0, keepdims=True))
        shifted = jnp.exp(logits - top)
        scale = jnp.exp(old - top)
        hit = lax.broadcasted_iota(jnp.int32, (WROWS, BOTH), 0) == toks[p, 0:1, :] - first
        acc[p, 0:1, :] = top
        acc[p, 1:2, :] = acc[p, 1:2, :] * scale + jnp.sum(shifted, axis=0, keepdims=True)
        acc[p, 2:3, :] = acc[p, 2:3, :] * scale + jnp.sum(shifted * logits, axis=0, keepdims=True)
        acc[p, 3:4, :] = acc[p, 3:4, :] + jnp.sum(jnp.where(hit, logits, 0.0), axis=0, keepdims=True)

    def run(pairs, slots):
        for p in pairs:
            for w in slots:
                chunk(p, w)

    def give(p):
        for half, d in enumerate((0, 4, 1, 7, 2, 6, 3, 5)[2 * p:2 * p + 2]):
            if d:
                send(f"a{d}", acc.at[p, :, pl.ds(half * ROWS, ROWS)], gathered.at[NZ - d], up(d))

    z_receive("S", 1)
    z_receive("A", 1)
    z_receive("S", 2)
    y_receive(1)

    weights_near(0)
    z_receive("A", 2)
    z_receive("S", 3)
    weights_near(1)
    y_finish(1)
    local_copies[1].wait()
    receive("w0", wts.at[4], sibling)
    run((1,), (0, 4))
    y_receive(2)
    z_receive("A", 3)
    z_receive("S", 4)
    y_finish(2)
    y_receive(3)

    for i in range(7):
        receive(f"k{i + 1}", all_squares.at[i + 1], sibling)
    square_sum = squares[...]
    for i in range(7):
        square_sum = square_sum + all_squares[i + 1]
    spread = jnp.sqrt(square_sum / (HD * 16) + NORM_EPS)
    places_row = jnp.concatenate([positions[0:1, :], positions[1:2, :]], axis=1).astype(jnp.float32)
    places = jnp.sum(picks * places_row, axis=1, keepdims=True)
    angles = places * freqs[0:1, :]
    turns = jnp.floor(angles * (0.5 / np.pi) + 0.5)
    angles = ((angles - turns * TWO_PI_1) - turns * TWO_PI_2) - turns * TWO_PI_3
    lanes = lax.broadcasted_iota(jnp.int32, (KPAD, HD), 1)
    cosine = jnp.cos(angles)
    sine = jnp.sin(angles)
    sine = jnp.where(lanes < HD // 2, -sine, sine)
    for head in range(2):
        values = projected[:, head * HD:(head + 1) * HD] / spread * key_gain[head:head + 1, :]
        turned = values * cosine + pltpu.roll(values, HD // 2, 1) * sine
        keys_out[:, head * HD:(head + 1) * HD] = turned[0:KROWS].astype(jnp.bfloat16)

    run((2,), (0, 4))
    weights_rest()
    z_receive("A", 4)
    y_receive(4)
    run((1,), (1, 2))
    weights_far(0)
    for first in (0, 2):
        from_sibling(1, first, 2)
        from_sibling(2, first, 2)
    run((1,), (5, 6))
    y_finish(3)
    run((2,), (1, 2, 5, 6))
    run((3,), (0, 4, 1, 2, 5, 6))
    y_finish(4)
    weights_far(1)
    run((0,), (0, 4, 1, 2, 5, 6))
    run((0, 3, 2, 1), (3,))
    for q in (0, 2, 1, 3):
        from_sibling(3, q, 1)
    for p in (0, 3, 2, 1):
        chunk(p, 7)
        give(p)

    gathered[0] = acc[0, :, 0:ROWS]
    for d in range(1, NZ):
        receive(f"a{d}", gathered.at[NZ - d], up(d))
    stats = merged(*(gathered[:, i, :] for i in range(4)))
    for i in range(4):
        part[i:i + 1, :] = stats[i]
    part[4:8, :] = jnp.zeros((4, ROWS), jnp.float32)
    mine = c * NY + y
    for i, peer in enumerate(voc_peers):
        send(f"v{i + 1}", part, parts.at[mine], peer)
    for i, peer in enumerate(partners):
        send(f"u{i}", part, parts.at[8 + mine], peer)
    parts[mine] = part[...]

    def place(d):
        source = lax.rem(voc + 8 - d, 8)
        return lax.rem(source, 2) * NY + lax.div(source, 2)

    for d in range(1, 8):
        receive(f"v{d}", parts.at[place(d)], sibling)
    receive("g", partner_segments, sibling)
    for d in range(8):
        receive(f"u{d}", parts.at[8 + place(d)], sibling)

    lane = lax.broadcasted_iota(jnp.int32, (1, ROWS), 1)
    seat = lax.broadcasted_iota(jnp.int32, (8, ROWS), 0)
    totals = []
    for first, group, labels in ((0, grp, segments), (8, partner, partner_segments)):
        length = lengths[group]
        sums = jnp.zeros((8, ROWS), jnp.float32)
        counts = jnp.zeros((8, ROWS), jnp.float32)
        last = jnp.zeros((1, ROWS), jnp.float32)
        for half in range(2):
            start = first + half * NY
            top, expsum, moment, picked = merged(*(parts[start:start + NY, i, :] for i in range(4)))
            logsum = top + jnp.log(expsum)
            slot = lane + half * ROWS
            live = slot < length
            logprob = jnp.where(live, picked - logsum, 0.0)
            label = labels[half:half + 1, :]
            if first == 0:
                logprob_out[half:half + 1, :] = logprob
                entropy_out[half:half + 1, :] = jnp.where(live, logsum - moment / expsum, 0.0)
            last = last + jnp.where(slot == length - 1, label.astype(jnp.float32), 0.0)
            member = seat == jnp.where(live, label, SEGS)
            sums = sums + jnp.where(member, logprob, 0.0)
            counts = counts + jnp.where(member, 1.0, 0.0)
        totals.append((
            jnp.sum(sums, axis=1, keepdims=True), jnp.sum(counts, axis=1, keepdims=True),
            jnp.sum(last, axis=1, keepdims=True),
        ))
    (sums, counts, last), (got_sums, got_counts, _) = totals
    row = lax.broadcasted_iota(jnp.int32, (8, 1), 0).astype(jnp.float32)
    even = lax.rem(x, 2) == 0
    joined = continues[grp - lax.rem(grp, 2)] == 1
    got_last = jnp.max(jnp.where((got_counts > 0) & (row < SEGS), row, 0.0), axis=0, keepdims=True)
    source = jnp.where(even, 0.0, got_last)
    target = jnp.where(even, last, 0.0)
    extra_sum = jnp.sum(jnp.where(row == source, got_sums, 0.0), axis=0, keepdims=True)
    extra_count = jnp.sum(jnp.where(row == source, got_counts, 0.0), axis=0, keepdims=True)
    update = joined & (row == target)
    total_sum = sums + jnp.where(update, extra_sum, 0.0)
    total_count = counts + jnp.where(update, extra_count, 0.0)
    means = total_sum / jnp.maximum(total_count, 1.0)
    mean_out[...] = jnp.sum(jnp.where(seat == lane, means, 0.0), axis=0, keepdims=True)[:, 0:SEGS]
    for copy in sent:
        copy.wait_send()


MESSAGES = 128


def local(
    final_hidden, norm_gain, head_weight, token_ids, group_lengths, segment_ids, continues,
    layer_input, key_weight, key_gain, positions, key_rows,
):
    steps = np.arange(HD // 2, dtype=np.float64)
    freqs = np.exp(-(2.0 * steps / HD) * np.log(ROPE_BASE)).astype(np.float32)
    freqs = jnp.asarray(np.concatenate([freqs, freqs])[None, :])
    anywhere = pl.BlockSpec(memory_space=pl.ANY)
    vmem = pl.BlockSpec(memory_space=pltpu.VMEM)
    smem = pl.BlockSpec(memory_space=pltpu.SMEM)
    f32, bf16 = jnp.float32, jnp.bfloat16
    logprob, entropy, mean, keys = pl.pallas_call(
        kernel,
        out_shape=(
            jax.ShapeDtypeStruct((2, ROWS), f32),
            jax.ShapeDtypeStruct((2, ROWS), f32),
            jax.ShapeDtypeStruct((1, SEGS), f32),
            jax.ShapeDtypeStruct((KROWS, BOTH), bf16),
        ),
        in_specs=[anywhere] * 4 + [vmem, vmem, smem, vmem, smem, vmem, vmem, smem, vmem],
        out_specs=(vmem,) * 4,
        scratch_shapes=[
            pltpu.VMEM((ROWS, DIM), bf16),
            pltpu.VMEM((8, DIM, ROWS), bf16),
            pltpu.VMEM((8, WROWS, DIM), bf16),
            pltpu.VMEM((2 * ROWS, DIM), bf16),
            pltpu.VMEM((DIM, BOTH), bf16),
            pltpu.VMEM((4, 1, BOTH), jnp.int32),
            pltpu.VMEM((4, 8, BOTH), f32),
            pltpu.VMEM((8, 8, ROWS), f32),
            pltpu.VMEM((8, ROWS), f32),
            pltpu.VMEM((16, 8, ROWS), f32),
            pltpu.VMEM((KPAD, HD), f32),
            pltpu.VMEM((8, KPAD, HD), f32),
            pltpu.VMEM((2, ROWS), jnp.int32),
            pltpu.SemaphoreType.DMA((4,)),
            pltpu.SemaphoreType.DMA((MESSAGES,)),
            pltpu.SemaphoreType.DMA((MESSAGES,)),
        ],
        compiler_params=pltpu.CompilerParams(
            collective_id=0, has_side_effects=True, vmem_limit_bytes=62 * 2**20
        ),
    )(
        final_hidden, head_weight, layer_input, key_weight,
        norm_gain.reshape(DIM // HD, HD), token_ids.reshape(-1, ROWS), group_lengths,
        segment_ids.reshape(2, ROWS), continues, key_gain.reshape(2, HD),
        positions.reshape(2, ROWS), key_rows, freqs,
    )
    return (logprob.reshape(-1), entropy.reshape(-1), mean.reshape(-1), keys)


def solution(mesh):
    in_specs = (
        P("grp", None),
        P(),
        P(("vocab", "grp"), None),
        P(),
        P(),
        P("grp"),
        P(),
        P("grp", None),
        P(None, "vocab"),
        P("vocab"),
        P("grp"),
        P("grp"),
    )
    out_specs = (P("grp"), P("grp"), P("grp"), P("grp", "vocab"))
    return jax.shard_map(local, mesh=mesh, in_specs=in_specs, out_specs=out_specs, check_vma=False)
```

```python
import jax
import jax.numpy as jnp
import numpy as np
from jax import lax
from jax.experimental import pallas as pl
from jax.experimental.pallas import tpu as pltpu
from jax.sharding import PartitionSpec as P

HD = 128
SEGS = 4
NORM_EPS = 1e-06
ROPE_BASE = 500000.0

NX, NY, NZ = 4, 4, 8
ROWS = 128
BOTH = 256
DIM = 2048
WROWS = 196
WPIECE = DIM // 4
SHARE = 320
ALONE = DIM - SHARE * NY
KROWS = 25
KPAD = 32
MESH = pl.DeviceIdType.MESH

TWO_PI_1 = 6.28125
TWO_PI_2 = float(np.float32(round((2 * np.pi - TWO_PI_1) * 2**20) / 2**20))
TWO_PI_3 = float(2 * np.pi - TWO_PI_1 - TWO_PI_2)


def place_of(d):
    return (0, 4, 1, 7, 2, 6, 3, 5).index(d)


def merged(maxes, sums, moments, picks):
    top = jnp.max(maxes, axis=0, keepdims=True)
    scale = jnp.exp(maxes - top)
    return (
        top,
        jnp.sum(sums * scale, axis=0, keepdims=True),
        jnp.sum(moments * scale, axis=0, keepdims=True),
        jnp.sum(picks, axis=0, keepdims=True),
    )


def kernel(
    hidden, weight, layer_input, key_weight,
    gain, tokens, lengths, segments, continues, key_gain, positions, key_rows, freqs,
    logprob_out, entropy_out, mean_out, keys_out,
    raw, held, wts, lin, kwt, toks, acc, gathered, part, parts,
    squares, all_squares, partner_segments,
    local_sems, send_sems, recv_sems,
):
    grp = lax.axis_index("grp")
    voc = lax.axis_index("vocab")
    x, z = lax.rem(grp, NX), lax.div(grp, NX)
    y, c = lax.div(voc, 2), lax.rem(voc, 2)

    def device(xx, yy, zz, cc):
        return (zz * NX + xx, yy * 2 + cc)

    def up(d):
        return device(x, y, lax.rem(z + d, NZ), c)

    x_up = device(lax.rem(x + 1, NX), y, z, c)
    x_down = device(lax.rem(x + NX - 1, NX), y, z, c)
    y_up = device(x, lax.rem(y + 1, NY), z, c)
    y_down = device(x, lax.rem(y + NY - 1, NY), z, c)
    sibling = device(x, y, z, 1 - c)
    partner = grp + 1 - 2 * lax.rem(x, 2)
    voc_peers = [(grp, lax.rem(voc + d, 8)) for d in range(1, 8)]

    ids = {}

    def remote(name, src, dst, to):
        number = ids.setdefault(name, len(ids))
        return pltpu.make_async_remote_copy(
            src_ref=src, dst_ref=dst, send_sem=send_sems.at[number], recv_sem=recv_sems.at[number],
            device_id=to, device_id_type=MESH,
        )

    sent = []

    def send(name, src, dst, to):
        copy = remote(name, src, dst, to)
        copy.start()
        sent.append(copy)

    def receive(name, dst, to):
        remote(name, dst, dst, to).wait_recv()

    local_copies = [
        pltpu.make_async_copy(hidden.at[pl.ds(pl.multiple_of(c * ROWS, ROWS), ROWS)], raw, local_sems.at[0]),
        pltpu.make_async_copy(weight, wts.at[0], local_sems.at[1]),
        pltpu.make_async_copy(layer_input, lin, local_sems.at[2]),
        pltpu.make_async_copy(key_weight, kwt, local_sems.at[3]),
    ]
    for copy in local_copies:
        copy.start()

    barrier = pltpu.get_barrier_semaphore()
    partners = [(partner, lax.rem(voc + d, 8)) for d in range(8)]
    other_x = device(lax.rem(x + 3 + 2 * lax.rem(x, 2), NX), y, z, c)
    peers = [up(d) for d in range(1, NZ)] + voc_peers + partners + [other_x]
    for peer in peers:
        pl.semaphore_signal(barrier, inc=1, device_id=peer, device_id_type=MESH)
    pl.semaphore_wait(barrier, len(peers))

    def piece(q):
        return pl.ds(q * WPIECE, WPIECE)

    def own_piece(way, first, count):
        cols = pl.ds(first * WPIECE, count * WPIECE)
        slot, to = (1, x_up) if way == "+" else (2, x_down)
        send(f"w{way}{first}", weight.at[:, cols], wts.at[slot, :, cols], to)

    own_piece("+", 0, 1)
    own_piece("-", 2, 1)

    def to_sibling(slot, first, count):
        cols = pl.ds(first * WPIECE, count * WPIECE)
        send(f"s{slot}{first}", wts.at[slot, :, cols], wts.at[4 + slot, :, cols], sibling)

    def from_sibling(slot, first, count):
        cols = pl.ds(first * WPIECE, count * WPIECE)
        receive(f"s{slot}{first}", wts.at[4 + slot, :, cols], sibling)

    def weights_near(i):
        receive(f"w+{i}", wts.at[1, :, piece(i)], x_up)
        send(f"wf+{i}", wts.at[1, :, piece(i)], wts.at[3, :, piece(i)], x_up)
        receive(f"w-{i + 2}", wts.at[2, :, piece(i + 2)], x_down)
        send(f"wf-{i + 2}", wts.at[2, :, piece(i + 2)], wts.at[3, :, piece(i + 2)], x_down)
        if i == 1:
            to_sibling(1, 0, 2)
            to_sibling(2, 2, 2)

    def weights_rest():
        cols = pl.ds(2 * WPIECE, 2 * WPIECE)
        receive("w+2", wts.at[1, :, cols], x_up)
        to_sibling(1, 2, 2)
        cols = pl.ds(0, 2 * WPIECE)
        receive("w-0", wts.at[2, :, cols], x_down)
        to_sibling(2, 0, 2)

    def weights_far(i):
        receive(f"wf+{i}", wts.at[3, :, piece(i)], x_up)
        to_sibling(3, i, 1)
        receive(f"wf-{i + 2}", wts.at[3, :, piece(i + 2)], x_down)
        to_sibling(3, i + 2, 1)

    local_copies[0].wait()
    total = jnp.zeros((ROWS, HD), jnp.float32)
    for j in range(DIM // HD):
        block = raw[:, j * HD:(j + 1) * HD].astype(jnp.float32)
        total = total + block * block
    inverse = lax.rsqrt(jnp.sum(total, axis=1, keepdims=True) / DIM + NORM_EPS)
    for j in range(DIM // HD):
        block = raw[:, j * HD:(j + 1) * HD].astype(jnp.float32)
        held[0, j * HD:(j + 1) * HD, :] = (block * inverse * gain[j:j + 1, :]).T.astype(jnp.bfloat16)

    def features(d, first, count):
        return held.at[place_of(d), pl.ds(first, count), :]

    def share(yy, first=0):
        return pl.multiple_of(ALONE + SHARE * lax.rem(yy, NY) + first, 16)

    LAST = {"S+": 3, "S-": 4, "A+": 4, "A-": 3, "B+": 4, "B-": 3}

    def away(way, k):
        return (NZ - k) % NZ if way == "+" else k

    def z_part(kind, d):
        if kind == "S":
            return features(d, share(y), SHARE)
        return features(d, 0 if kind == "A" else ALONE // 2, ALONE // 2)

    def z_send(kind, way, k):
        send(
            f"z{kind}{way}{k}", z_part(kind, away(way, k - 1)), z_part(kind, away(way, k)),
            up(1) if way == "+" else up(NZ - 1),
        )

    def z_receive(kind, k):
        for way in "+-":
            if k > LAST[kind + way]:
                continue
            d = away(way, k)
            receive(f"z{kind}{way}{k}", z_part(kind, d), up(1))
            if k < LAST[kind + way]:
                z_send(kind, way, k + 1)
        if kind == "S":
            ref = shares(k, share(y), SHARE)
            send(f"y+{k}", ref, ref, y_up)
            send(f"y-{k}", ref, ref, y_down)

    def shares(k, first, count):
        slots = pl.ds(2 * k, 2) if k < 4 else pl.ds(1, 1)
        return held.at[slots, pl.ds(first, count), :]

    half_share = SHARE // 2

    def y_receive(k):
        below, above = y + NY - 1, y + 1
        receive(f"y+{k}", shares(k, share(below), SHARE), y_up)
        ref = shares(k, share(below), half_share)
        send(f"yf+{k}", ref, ref, y_up)
        receive(f"y-{k}", shares(k, share(above), SHARE), y_down)
        ref = shares(k, share(above, half_share), half_share)
        send(f"yf-{k}", ref, ref, y_down)

    def y_finish(k):
        receive(f"yf+{k}", shares(k, share(y + 2), half_share), y_up)
        receive(f"yf-{k}", shares(k, share(y + 2, half_share), half_share), y_down)

    def z_start(kinds):
        for kind in kinds:
            for way in "+-":
                z_send(kind, way, 1)

    z_start(FIRST)
    own_piece("+", 1, 1)
    own_piece("-", 3, 1)
    own_piece("+", 2, 2)
    own_piece("-", 0, 2)
    send("w0", weight, wts.at[4], sibling)
    send("g", segments, partner_segments, partners[0])

    row_ids = lax.broadcasted_iota(jnp.int32, (KPAD, BOTH), 0)
    col_ids = lax.broadcasted_iota(jnp.int32, (KPAD, BOTH), 1)
    wanted = jnp.zeros((KPAD, BOTH), jnp.int32)
    for i in range(KROWS):
        wanted = jnp.where(row_ids == i, key_rows[i], wanted)
    picks = jnp.where(col_ids == wanted, 1.0, 0.0)
    local_copies[2].wait()
    local_copies[3].wait()
    chosen = jnp.dot(picks.astype(jnp.bfloat16), lin[...], preferred_element_type=jnp.float32)
    projected = jnp.dot(chosen.astype(jnp.bfloat16), kwt[...], preferred_element_type=jnp.float32)
    squares[...] = jnp.broadcast_to(jnp.sum(projected * projected, axis=1, keepdims=True), (KPAD, HD))
    for i, peer in enumerate(voc_peers):
        send(f"k{i + 1}", squares, all_squares.at[i + 1], peer)

    for p in range(4):
        acc[p, 0:1, :] = jnp.full((1, BOTH), -jnp.inf, jnp.float32)
        acc[p, 1:8, :] = jnp.zeros((7, BOTH), jnp.float32)
        for half, d in enumerate((0, 4, 1, 7, 2, 6, 3, 5)[2 * p:2 * p + 2]):
            row = (lax.rem(z + d, NZ) * NX + x) * 2 + c
            toks[p, 0:1, half * ROWS:(half + 1) * ROWS] = tokens[pl.ds(row, 1), :]

    def chunk(p, w):
        other, turn = divmod(w, 4)
        shift = (0, NX - 1, 1, 2)[turn]
        first = (y * 2 + lax.rem(c + other, 2)) * (WROWS * NX * NZ) + (z * NX + lax.rem(x + shift, NX)) * WROWS
        logits = lax.dot_general(
            wts[w], jnp.concatenate([held[2 * p], held[2 * p + 1]], axis=1),
            (((1,), (0,)), ((), ())), preferred_element_type=jnp.float32
        ).astype(jnp.bfloat16).astype(jnp.float32)
        old = acc[p, 0:1, :]
        top = jnp.maximum(old, jnp.max(logits, axis=0, keepdims=True))
        shifted = jnp.exp(logits - top)
        scale = jnp.exp(old - top)
        hit = lax.broadcasted_iota(jnp.int32, (WROWS, BOTH), 0) == toks[p, 0:1, :] - first
        acc[p, 0:1, :] = top
        acc[p, 1:2, :] = acc[p, 1:2, :] * scale + jnp.sum(shifted, axis=0, keepdims=True)
        acc[p, 2:3, :] = acc[p, 2:3, :] * scale + jnp.sum(shifted * logits, axis=0, keepdims=True)
        acc[p, 3:4, :] = acc[p, 3:4, :] + jnp.sum(jnp.where(hit, logits, 0.0), axis=0, keepdims=True)

    def run(pairs, slots):
        for p in pairs:
            for w in slots:
                chunk(p, w)

    def give(p):
        for half, d in enumerate((0, 4, 1, 7, 2, 6, 3, 5)[2 * p:2 * p + 2]):
            if d:
                send(f"a{d}", acc.at[p, :, pl.ds(half * ROWS, ROWS)], gathered.at[NZ - d], up(d))

    def finish_keys():
        for i in range(7):
            receive(f"k{i + 1}", all_squares.at[i + 1], sibling)
        square_sum = squares[...]
        for i in range(7):
            square_sum = square_sum + all_squares[i + 1]
        spread = jnp.sqrt(square_sum / (HD * 16) + NORM_EPS)
        places_row = jnp.concatenate([positions[0:1, :], positions[1:2, :]], axis=1).astype(jnp.float32)
        places = jnp.sum(picks * places_row, axis=1, keepdims=True)
        angles = places * freqs[0:1, :]
        turns = jnp.floor(angles * (0.5 / np.pi) + 0.5)
        angles = ((angles - turns * TWO_PI_1) - turns * TWO_PI_2) - turns * TWO_PI_3
        lanes = lax.broadcasted_iota(jnp.int32, (KPAD, HD), 1)
        cosine = jnp.cos(angles)
        sine = jnp.sin(angles)
        sine = jnp.where(lanes < HD // 2, -sine, sine)
        for head in range(2):
            values = projected[:, head * HD:(head + 1) * HD] / spread * key_gain[head:head + 1, :]
            turned = values * cosine + pltpu.roll(values, HD // 2, 1) * sine
            keys_out[:, head * HD:(head + 1) * HD] = turned[0:KROWS].astype(jnp.bfloat16)

    def start_chunks():
        local_copies[1].wait()
        receive("w0", wts.at[4], sibling)

    def near_from_sibling():
        for first in (0, 2):
            from_sibling(1, first, 2)
            from_sibling(2, first, 2)

    def far_from_sibling():
        for q in (0, 2, 1, 3):
            from_sibling(3, q, 1)

    def last_chunk(p):
        chunk(p, 7)
        give(p)

    marks = []

    def settle():
        for copy in sent[:marks[0]]:
            copy.wait_send()
        del sent[:marks[0]]

    events = {
        "M": lambda: marks.append(len(sent)), "w": settle,
        "S": lambda k: z_receive("S", k), "A": lambda k: z_receive("A", k),
        "B": lambda k: z_receive("B", k), "a": z_start,
        "Y": y_receive, "F": y_finish, "K": finish_keys,
        "n": weights_near, "r": weights_rest, "f": weights_far,
        "o": start_chunks, "m": near_from_sibling, "l": far_from_sibling,
        "C": run, "L": last_chunk,
    }
    for name, *rest in ORDER:
        events[name](*rest)

    gathered[0] = acc[0, :, 0:ROWS]
    for d in range(1, NZ):
        receive(f"a{d}", gathered.at[NZ - d], up(d))
    stats = merged(*(gathered[:, i, :] for i in range(4)))
    for i in range(4):
        part[i:i + 1, :] = stats[i]
    part[4:8, :] = jnp.zeros((4, ROWS), jnp.float32)
    mine = c * NY + y
    for d in (4, 3, 5, 2, 6, 0, 1, 7):
        send(f"u{d}", part, parts.at[8 + mine], partners[d])
        if d:
            send(f"v{d}", part, parts.at[mine], voc_peers[d - 1])
    parts[mine] = part[...]

    def place(d):
        source = lax.rem(voc + 8 - d, 8)
        return lax.rem(source, 2) * NY + lax.div(source, 2)

    for d in range(1, 8):
        receive(f"v{d}", parts.at[place(d)], sibling)
    receive("g", partner_segments, sibling)
    for d in range(8):
        receive(f"u{d}", parts.at[8 + place(d)], sibling)

    lane = lax.broadcasted_iota(jnp.int32, (1, ROWS), 1)
    seat = lax.broadcasted_iota(jnp.int32, (8, ROWS), 0)
    totals = []
    for first, group, labels in ((0, grp, segments), (8, partner, partner_segments)):
        length = lengths[group]
        sums = jnp.zeros((8, ROWS), jnp.float32)
        counts = jnp.zeros((8, ROWS), jnp.float32)
        last = jnp.zeros((1, ROWS), jnp.float32)
        for half in range(2):
            start = first + half * NY
            top, expsum, moment, picked = merged(*(parts[start:start + NY, i, :] for i in range(4)))
            logsum = top + jnp.log(expsum)
            slot = lane + half * ROWS
            live = slot < length
            logprob = jnp.where(live, picked - logsum, 0.0)
            label = labels[half:half + 1, :]
            if first == 0:
                logprob_out[half:half + 1, :] = logprob
                entropy_out[half:half + 1, :] = jnp.where(live, logsum - moment / expsum, 0.0)
            last = last + jnp.where(slot == length - 1, label.astype(jnp.float32), 0.0)
            member = seat == jnp.where(live, label, SEGS)
            sums = sums + jnp.where(member, logprob, 0.0)
            counts = counts + jnp.where(member, 1.0, 0.0)
        totals.append((
            jnp.sum(sums, axis=1, keepdims=True), jnp.sum(counts, axis=1, keepdims=True),
            jnp.sum(last, axis=1, keepdims=True),
        ))
    (sums, counts, last), (got_sums, got_counts, _) = totals
    row = lax.broadcasted_iota(jnp.int32, (8, 1), 0).astype(jnp.float32)
    even = lax.rem(x, 2) == 0
    joined = continues[grp - lax.rem(grp, 2)] == 1
    got_last = jnp.max(jnp.where((got_counts > 0) & (row < SEGS), row, 0.0), axis=0, keepdims=True)
    source = jnp.where(even, 0.0, got_last)
    target = jnp.where(even, last, 0.0)
    extra_sum = jnp.sum(jnp.where(row == source, got_sums, 0.0), axis=0, keepdims=True)
    extra_count = jnp.sum(jnp.where(row == source, got_counts, 0.0), axis=0, keepdims=True)
    update = joined & (row == target)
    total_sum = sums + jnp.where(update, extra_sum, 0.0)
    total_count = counts + jnp.where(update, extra_count, 0.0)
    means = total_sum / jnp.maximum(total_count, 1.0)
    mean_out[...] = jnp.sum(jnp.where(seat == lane, means, 0.0), axis=0, keepdims=True)[:, 0:SEGS]
    for copy in sent:
        copy.wait_send()


MESSAGES = 128
MOST = (0, 4, 1, 2, 5, 6)
FIRST = "SAB"
ORDER = [("S", 1), ("A", 1), ("B", 1), ("S", 2), ("Y", 1), ("n", 0), ("A", 2), ("B", 2), ("S", 3), ("n", 1), ("F", 1),
    ("o",), ("Y", 2), ("A", 3), ("B", 3), ("S", 4), ("C", (1,), (0, 4)), ("F", 2), ("Y", 3), ("C", (2,), (0, 4)), ("K",), ("r",), ("A", 4), ("B", 4), ("C", (1,), (1, 2)), ("Y", 4), ("m",), ("C", (1,), (5, 6)), ("C", (2,), (1, 2, 5, 6)), ("M",), ("f", 0), ("F", 3), ("C", (3,), MOST), ("w",), ("f", 1), ("C", (3, 2, 1), (3,)), ("F", 4), ("C", (0,), MOST), ("C", (0,), (3,)), ("l",), ("L", 0), ("L", 3), ("L", 2), ("L", 1),
]


def local(
    final_hidden, norm_gain, head_weight, token_ids, group_lengths, segment_ids, continues,
    layer_input, key_weight, key_gain, positions, key_rows,
):
    steps = np.arange(HD // 2, dtype=np.float64)
    freqs = np.exp(-(2.0 * steps / HD) * np.log(ROPE_BASE)).astype(np.float32)
    freqs = jnp.asarray(np.concatenate([freqs, freqs])[None, :])
    anywhere = pl.BlockSpec(memory_space=pl.ANY)
    vmem = pl.BlockSpec(memory_space=pltpu.VMEM)
    smem = pl.BlockSpec(memory_space=pltpu.SMEM)
    f32, bf16 = jnp.float32, jnp.bfloat16
    logprob, entropy, mean, keys = pl.pallas_call(
        kernel,
        out_shape=(
            jax.ShapeDtypeStruct((2, ROWS), f32),
            jax.ShapeDtypeStruct((2, ROWS), f32),
            jax.ShapeDtypeStruct((1, SEGS), f32),
            jax.ShapeDtypeStruct((KROWS, BOTH), bf16),
        ),
        in_specs=[anywhere] * 4 + [vmem, vmem, smem, vmem, smem, vmem, vmem, smem, vmem],
        out_specs=(vmem,) * 4,
        scratch_shapes=[
            pltpu.VMEM((ROWS, DIM), bf16),
            pltpu.VMEM((8, DIM, ROWS), bf16),
            pltpu.VMEM((8, WROWS, DIM), bf16),
            pltpu.VMEM((2 * ROWS, DIM), bf16),
            pltpu.VMEM((DIM, BOTH), bf16),
            pltpu.VMEM((4, 1, BOTH), jnp.int32),
            pltpu.VMEM((4, 8, BOTH), f32),
            pltpu.VMEM((8, 8, ROWS), f32),
            pltpu.VMEM((8, ROWS), f32),
            pltpu.VMEM((16, 8, ROWS), f32),
            pltpu.VMEM((KPAD, HD), f32),
            pltpu.VMEM((8, KPAD, HD), f32),
            pltpu.VMEM((2, ROWS), jnp.int32),
            pltpu.SemaphoreType.DMA((4,)),
            pltpu.SemaphoreType.DMA((MESSAGES,)),
            pltpu.SemaphoreType.DMA((MESSAGES,)),
        ],
        compiler_params=pltpu.CompilerParams(
            collective_id=0, has_side_effects=True, vmem_limit_bytes=62 * 2**20
        ),
    )(
        final_hidden, head_weight, layer_input, key_weight,
        norm_gain.reshape(DIM // HD, HD), token_ids.reshape(-1, ROWS), group_lengths,
        segment_ids.reshape(2, ROWS), continues, key_gain.reshape(2, HD),
        positions.reshape(2, ROWS), key_rows, freqs,
    )
    outs = (logprob, entropy, mean, keys)

    def finish(*refs):
        copies = [pltpu.make_async_copy(refs[i], refs[4 + i], refs[8].at[i]) for i in range(4)]
        for copy in copies:
            copy.start()
        for copy in copies:
            copy.wait()

    logprob, entropy, mean, keys = pl.pallas_call(
        finish,
        out_shape=tuple(jax.ShapeDtypeStruct(a.shape, a.dtype) for a in outs),
        in_specs=[anywhere] * 4,
        out_specs=(anywhere,) * 4,
        scratch_shapes=[pltpu.SemaphoreType.DMA((4,))],
    )(*outs)
    return (logprob.reshape(-1), entropy.reshape(-1), mean.reshape(-1), keys)


def solution(mesh):
    in_specs = (
        P("grp", None),
        P(),
        P(("vocab", "grp"), None),
        P(),
        P(),
        P("grp"),
        P(),
        P("grp", None),
        P(None, "vocab"),
        P("vocab"),
        P("grp"),
        P("grp"),
    )
    out_specs = (P("grp"), P("grp"), P("grp"), P("grp", "vocab"))
    return jax.shard_map(local, mesh=mesh, in_specs=in_specs, out_specs=out_specs, check_vma=False)
```

```python
import jax
import jax.numpy as jnp
import numpy as np
from jax import lax
from jax.experimental import pallas as pl
from jax.experimental.pallas import tpu as pltpu
from jax.sharding import PartitionSpec as P

HD = 128
SEGS = 4
NORM_EPS = 1e-06
ROPE_BASE = 500000.0

NX, NY, NZ = 4, 4, 8
ROWS = 128
BOTH = 256
DIM = 2048
WROWS = 196
WPIECE = DIM // 4
SHARE = 352
ALONE = DIM - SHARE * NY
KROWS = 25
KPAD = 32
MESH = pl.DeviceIdType.MESH

TWO_PI_1 = 6.28125
TWO_PI_2 = float(np.float32(round((2 * np.pi - TWO_PI_1) * 2**20) / 2**20))
TWO_PI_3 = float(2 * np.pi - TWO_PI_1 - TWO_PI_2)


def place_of(d):
    return (0, 4, 1, 7, 2, 6, 3, 5).index(d)


def merged(maxes, sums, moments, picks):
    top = jnp.max(maxes, axis=0, keepdims=True)
    scale = jnp.exp(maxes - top)
    return (
        top,
        jnp.sum(sums * scale, axis=0, keepdims=True),
        jnp.sum(moments * scale, axis=0, keepdims=True),
        jnp.sum(picks, axis=0, keepdims=True),
    )


def kernel(
    hidden, weight, layer_input, key_weight,
    gain_in, tokens_in, segments_in, key_gain_in, positions_in, freqs_in, lengths, continues, key_rows,
    logprob_to, entropy_to, mean_to, keys_to,
    gain, tokens, segments, key_gain, positions, freqs, logprob_out, entropy_out, mean_out, keys_out,
    raw, held, wts, lin, kwt, toks, acc, gathered, part, parts,
    squares, all_squares, partner_segments,
    local_sems, send_sems, recv_sems,
):
    grp = lax.axis_index("grp")
    voc = lax.axis_index("vocab")
    x, z = lax.rem(grp, NX), lax.div(grp, NX)
    y, c = lax.div(voc, 2), lax.rem(voc, 2)

    def device(xx, yy, zz, cc):
        return (zz * NX + xx, yy * 2 + cc)

    def up(d):
        return device(x, y, lax.rem(z + d, NZ), c)

    x_up = device(lax.rem(x + 1, NX), y, z, c)
    x_down = device(lax.rem(x + NX - 1, NX), y, z, c)
    y_up = device(x, lax.rem(y + 1, NY), z, c)
    y_down = device(x, lax.rem(y + NY - 1, NY), z, c)
    sibling = device(x, y, z, 1 - c)
    partner = grp + 1 - 2 * lax.rem(x, 2)
    voc_peers = [(grp, lax.rem(voc + d, 8)) for d in range(1, 8)]

    ids = {}

    def remote(name, src, dst, to):
        number = ids.setdefault(name, len(ids))
        return pltpu.make_async_remote_copy(
            src_ref=src, dst_ref=dst, send_sem=send_sems.at[number], recv_sem=recv_sems.at[number],
            device_id=to, device_id_type=MESH,
        )

    sent = []

    def send(name, src, dst, to):
        copy = remote(name, src, dst, to)
        copy.start()
        sent.append(copy)

    def receive(name, dst, to):
        remote(name, dst, dst, to).wait_recv()

    local_copies = [
        pltpu.make_async_copy(hidden.at[pl.ds(pl.multiple_of(c * ROWS, ROWS), ROWS)], raw, local_sems.at[0]),
        pltpu.make_async_copy(weight, wts.at[0], local_sems.at[1]),
        pltpu.make_async_copy(layer_input, lin, local_sems.at[2]),
        pltpu.make_async_copy(key_weight, kwt, local_sems.at[3]),
    ]
    small = [
        pltpu.make_async_copy(src, dst, local_sems.at[4 + i]) for i, (src, dst) in enumerate((
            (gain_in, gain), (tokens_in, tokens), (segments_in, segments),
            (key_gain_in, key_gain), (positions_in, positions), (freqs_in, freqs),
        ))
    ]
    results = [
        pltpu.make_async_copy(src, dst, local_sems.at[10 + i]) for i, (src, dst) in enumerate((
            (logprob_out, logprob_to), (entropy_out, entropy_to), (mean_out, mean_to), (keys_out, keys_to),
        ))
    ]

    barrier = pltpu.get_barrier_semaphore()
    partners = [(partner, lax.rem(voc + d, 8)) for d in range(8)]
    other_x = device(lax.rem(x + 3 + 2 * lax.rem(x, 2), NX), y, z, c)
    peers = [other_x] + partners + [up(d) for d in (1, 7, 2, 6, 3, 5, 4)] + voc_peers
    for peer in peers:
        pl.semaphore_signal(barrier, inc=1, device_id=peer, device_id_type=MESH)
    for copy in local_copies[:1] + small + local_copies[1:]:
        copy.start()
    pl.semaphore_wait(barrier, len(peers))

    def piece(q):
        return pl.ds(q * WPIECE, WPIECE)

    def own_piece(way, first, count):
        cols = pl.ds(first * WPIECE, count * WPIECE)
        slot, to = (1, x_up) if way == "+" else (2, x_down)
        send(f"w{way}{first}", weight.at[:, cols], wts.at[slot, :, cols], to)

    own_piece("+", 0, 1)
    own_piece("-", 2, 1)

    def to_sibling(slot, first, count):
        cols = pl.ds(first * WPIECE, count * WPIECE)
        send(f"s{slot}{first}", wts.at[slot, :, cols], wts.at[4 + slot, :, cols], sibling)

    def from_sibling(slot, first, count):
        cols = pl.ds(first * WPIECE, count * WPIECE)
        receive(f"s{slot}{first}", wts.at[4 + slot, :, cols], sibling)

    def weights_near(i):
        receive(f"w+{i}", wts.at[1, :, piece(i)], x_up)
        send(f"wf+{i}", wts.at[1, :, piece(i)], wts.at[3, :, piece(i)], x_up)
        receive(f"w-{i + 2}", wts.at[2, :, piece(i + 2)], x_down)
        send(f"wf-{i + 2}", wts.at[2, :, piece(i + 2)], wts.at[3, :, piece(i + 2)], x_down)
        if i == 1:
            to_sibling(1, 0, 2)
            to_sibling(2, 2, 2)

    def weights_rest():
        cols = pl.ds(2 * WPIECE, 2 * WPIECE)
        receive("w+2", wts.at[1, :, cols], x_up)
        to_sibling(1, 2, 2)
        cols = pl.ds(0, 2 * WPIECE)
        receive("w-0", wts.at[2, :, cols], x_down)
        to_sibling(2, 0, 2)

    def weights_far(i):
        receive(f"wf+{i}", wts.at[3, :, piece(i)], x_up)
        to_sibling(3, i, 1)
        receive(f"wf-{i + 2}", wts.at[3, :, piece(i + 2)], x_down)
        to_sibling(3, i + 2, 1)

    local_copies[0].wait()
    small[0].wait()
    total = jnp.zeros((ROWS, HD), jnp.float32)
    for j in range(DIM // HD):
        block = raw[:, j * HD:(j + 1) * HD].astype(jnp.float32)
        total = total + block * block
    inverse = lax.rsqrt(jnp.sum(total, axis=1, keepdims=True) / DIM + NORM_EPS)
    for j in range(DIM // HD):
        block = raw[:, j * HD:(j + 1) * HD].astype(jnp.float32)
        held[0, j * HD:(j + 1) * HD, :] = (block * inverse * gain[j:j + 1, :]).T.astype(jnp.bfloat16)

    def features(d, first, count):
        return held.at[place_of(d), pl.ds(first, count), :]

    def share(yy, first=0):
        return pl.multiple_of(ALONE + SHARE * lax.rem(yy, NY) + first, 16)

    LAST = {"S+": 3, "S-": 4, "A+": 4, "A-": 3, "B+": 4, "B-": 3}

    def away(way, k):
        return (NZ - k) % NZ if way == "+" else k

    def z_part(kind, d):
        if kind == "S":
            return features(d, share(y), SHARE)
        return features(d, 0 if kind == "A" else ALONE // 2, ALONE // 2)

    def z_send(kind, way, k):
        send(
            f"z{kind}{way}{k}", z_part(kind, away(way, k - 1)), z_part(kind, away(way, k)),
            up(1) if way == "+" else up(NZ - 1),
        )

    def z_receive(kind, k):
        for way in "+-":
            if k > LAST[kind + way]:
                continue
            d = away(way, k)
            receive(f"z{kind}{way}{k}", z_part(kind, d), up(1))
            if k < LAST[kind + way]:
                z_send(kind, way, k + 1)
        if kind == "S":
            ref = shares(k, share(y), SHARE)
            send(f"y+{k}", ref, ref, y_up)
            send(f"y-{k}", ref, ref, y_down)

    def shares(k, first, count):
        slots = pl.ds(2 * k, 2) if k < 4 else pl.ds(1, 1)
        return held.at[slots, pl.ds(first, count), :]

    half_share = SHARE // 2

    def y_receive(k):
        below, above = y + NY - 1, y + 1
        receive(f"y+{k}", shares(k, share(below), SHARE), y_up)
        ref = shares(k, share(below), half_share)
        send(f"yf+{k}", ref, ref, y_up)
        receive(f"y-{k}", shares(k, share(above), SHARE), y_down)
        ref = shares(k, share(above, half_share), half_share)
        send(f"yf-{k}", ref, ref, y_down)

    def y_finish(k):
        receive(f"yf+{k}", shares(k, share(y + 2), half_share), y_up)
        receive(f"yf-{k}", shares(k, share(y + 2, half_share), half_share), y_down)

    def z_start(kinds):
        for kind in kinds:
            for way in "+-":
                z_send(kind, way, 1)

    z_start(FIRST)
    own_piece("+", 1, 1)
    own_piece("-", 3, 1)
    own_piece("+", 2, 2)
    own_piece("-", 0, 2)
    send("w0", weight, wts.at[4], sibling)
    for copy in small[1:]:
        copy.wait()
    send("g", segments, partner_segments, partners[0])

    row_ids = lax.broadcasted_iota(jnp.int32, (KPAD, BOTH), 0)
    col_ids = lax.broadcasted_iota(jnp.int32, (KPAD, BOTH), 1)
    wanted = jnp.zeros((KPAD, BOTH), jnp.int32)
    for i in range(KROWS):
        wanted = jnp.where(row_ids == i, key_rows[i], wanted)
    picks = jnp.where(col_ids == wanted, 1.0, 0.0)
    local_copies[2].wait()
    local_copies[3].wait()
    chosen = jnp.dot(picks.astype(jnp.bfloat16), lin[...], preferred_element_type=jnp.float32)
    projected = jnp.dot(chosen.astype(jnp.bfloat16), kwt[...], preferred_element_type=jnp.float32)
    squares[...] = jnp.broadcast_to(jnp.sum(projected * projected, axis=1, keepdims=True), (KPAD, HD))
    for i, peer in enumerate(voc_peers):
        send(f"k{i + 1}", squares, all_squares.at[i + 1], peer)

    for p in range(4):
        acc[p, 0:1, :] = jnp.full((1, BOTH), -jnp.inf, jnp.float32)
        acc[p, 1:8, :] = jnp.zeros((7, BOTH), jnp.float32)
        for half, d in enumerate((0, 4, 1, 7, 2, 6, 3, 5)[2 * p:2 * p + 2]):
            row = (lax.rem(z + d, NZ) * NX + x) * 2 + c
            toks[p, 0:1, half * ROWS:(half + 1) * ROWS] = tokens[pl.ds(row, 1), :]

    def chunk(p, w):
        other, turn = divmod(w, 4)
        shift = (0, NX - 1, 1, 2)[turn]
        first = (y * 2 + lax.rem(c + other, 2)) * (WROWS * NX * NZ) + (z * NX + lax.rem(x + shift, NX)) * WROWS
        logits = lax.dot_general(
            wts[w], jnp.concatenate([held[2 * p], held[2 * p + 1]], axis=1),
            (((1,), (0,)), ((), ())), preferred_element_type=jnp.float32
        ).astype(jnp.bfloat16).astype(jnp.float32)
        old = acc[p, 0:1, :]
        top = jnp.maximum(old, jnp.max(logits, axis=0, keepdims=True))
        shifted = jnp.exp(logits - top)
        scale = jnp.exp(old - top)
        hit = lax.broadcasted_iota(jnp.int32, (WROWS, BOTH), 0) == toks[p, 0:1, :] - first
        acc[p, 0:1, :] = top
        acc[p, 1:2, :] = acc[p, 1:2, :] * scale + jnp.sum(shifted, axis=0, keepdims=True)
        acc[p, 2:3, :] = acc[p, 2:3, :] * scale + jnp.sum(shifted * logits, axis=0, keepdims=True)
        acc[p, 3:4, :] = acc[p, 3:4, :] + jnp.sum(jnp.where(hit, logits, 0.0), axis=0, keepdims=True)

    def run(pairs, slots):
        for p in pairs:
            for w in slots:
                chunk(p, w)

    def give(p):
        for half, d in enumerate((0, 4, 1, 7, 2, 6, 3, 5)[2 * p:2 * p + 2]):
            if d:
                send(f"a{d}", acc.at[p, :, pl.ds(half * ROWS, ROWS)], gathered.at[NZ - d], up(d))

    def finish_keys():
        for i in range(7):
            receive(f"k{i + 1}", all_squares.at[i + 1], sibling)
        square_sum = squares[...]
        for i in range(7):
            square_sum = square_sum + all_squares[i + 1]
        spread = jnp.sqrt(square_sum / (HD * 16) + NORM_EPS)
        places_row = jnp.concatenate([positions[0:1, :], positions[1:2, :]], axis=1).astype(jnp.float32)
        places = jnp.sum(picks * places_row, axis=1, keepdims=True)
        angles = places * freqs[0:1, :]
        turns = jnp.floor(angles * (0.5 / np.pi) + 0.5)
        angles = ((angles - turns * TWO_PI_1) - turns * TWO_PI_2) - turns * TWO_PI_3
        lanes = lax.broadcasted_iota(jnp.int32, (KPAD, HD), 1)
        cosine = jnp.cos(angles)
        sine = jnp.sin(angles)
        sine = jnp.where(lanes < HD // 2, -sine, sine)
        for head in range(2):
            values = projected[:, head * HD:(head + 1) * HD] / spread * key_gain[head:head + 1, :]
            turned = values * cosine + pltpu.roll(values, HD // 2, 1) * sine
            keys_out[:, head * HD:(head + 1) * HD] = turned[0:KROWS].astype(jnp.bfloat16)

        results[3].start()

    def start_chunks():
        local_copies[1].wait()
        receive("w0", wts.at[4], sibling)

    def near_from_sibling():
        for first in (0, 2):
            from_sibling(1, first, 2)
            from_sibling(2, first, 2)

    def far_from_sibling():
        for q in (0, 2, 1, 3):
            from_sibling(3, q, 1)

    def last_chunk(p):
        chunk(p, 7)
        give(p)

    marks = []

    def settle():
        for copy in sent[:marks[0]]:
            copy.wait_send()
        del sent[:marks[0]]

    events = {
        "M": lambda: marks.append(len(sent)), "w": settle,
        "S": lambda k: z_receive("S", k), "A": lambda k: z_receive("A", k),
        "B": lambda k: z_receive("B", k), "a": z_start,
        "Y": y_receive, "F": y_finish, "K": finish_keys,
        "n": weights_near, "r": weights_rest, "f": weights_far,
        "o": start_chunks, "m": near_from_sibling, "l": far_from_sibling,
        "C": run, "L": last_chunk,
    }
    for name, *rest in ORDER:
        events[name](*rest)

    gathered[0] = acc[0, :, 0:ROWS]
    for d in range(1, NZ):
        receive(f"a{d}", gathered.at[NZ - d], up(d))
    stats = merged(*(gathered[:, i, :] for i in range(4)))
    for i in range(4):
        part[i:i + 1, :] = stats[i]
    part[4:8, :] = jnp.zeros((4, ROWS), jnp.float32)
    mine = c * NY + y
    for d in (4, 3, 5, 2, 6, 0, 1, 7):
        send(f"u{d}", part, parts.at[8 + mine], partners[d])
        if d:
            send(f"v{d}", part, parts.at[mine], voc_peers[d - 1])
    parts[mine] = part[...]

    def place(d):
        source = lax.rem(voc + 8 - d, 8)
        return lax.rem(source, 2) * NY + lax.div(source, 2)

    for d in range(1, 8):
        receive(f"v{d}", parts.at[place(d)], sibling)
    receive("g", partner_segments, sibling)
    for d in range(8):
        receive(f"u{d}", parts.at[8 + place(d)], sibling)

    lane = lax.broadcasted_iota(jnp.int32, (1, ROWS), 1)
    seat = lax.broadcasted_iota(jnp.int32, (8, ROWS), 0)
    totals = []
    for first, group, labels in ((0, grp, segments), (8, partner, partner_segments)):
        length = lengths[group]
        sums = jnp.zeros((8, ROWS), jnp.float32)
        counts = jnp.zeros((8, ROWS), jnp.float32)
        last = jnp.zeros((1, ROWS), jnp.float32)
        for half in range(2):
            start = first + half * NY
            top, expsum, moment, picked = merged(*(parts[start:start + NY, i, :] for i in range(4)))
            logsum = top + jnp.log(expsum)
            slot = lane + half * ROWS
            live = slot < length
            logprob = jnp.where(live, picked - logsum, 0.0)
            label = labels[half:half + 1, :]
            if first == 0:
                logprob_out[half:half + 1, :] = logprob
                entropy_out[half:half + 1, :] = jnp.where(live, logsum - moment / expsum, 0.0)
            last = last + jnp.where(slot == length - 1, label.astype(jnp.float32), 0.0)
            member = seat == jnp.where(live, label, SEGS)
            sums = sums + jnp.where(member, logprob, 0.0)
            counts = counts + jnp.where(member, 1.0, 0.0)
        totals.append((
            jnp.sum(sums, axis=1, keepdims=True), jnp.sum(counts, axis=1, keepdims=True),
            jnp.sum(last, axis=1, keepdims=True),
        ))
    (sums, counts, last), (got_sums, got_counts, _) = totals
    row = lax.broadcasted_iota(jnp.int32, (8, 1), 0).astype(jnp.float32)
    even = lax.rem(x, 2) == 0
    joined = continues[grp - lax.rem(grp, 2)] == 1
    got_last = jnp.max(jnp.where((got_counts > 0) & (row < SEGS), row, 0.0), axis=0, keepdims=True)
    source = jnp.where(even, 0.0, got_last)
    target = jnp.where(even, last, 0.0)
    extra_sum = jnp.sum(jnp.where(row == source, got_sums, 0.0), axis=0, keepdims=True)
    extra_count = jnp.sum(jnp.where(row == source, got_counts, 0.0), axis=0, keepdims=True)
    update = joined & (row == target)
    total_sum = sums + jnp.where(update, extra_sum, 0.0)
    total_count = counts + jnp.where(update, extra_count, 0.0)
    means = total_sum / jnp.maximum(total_count, 1.0)
    mean_out[...] = jnp.sum(jnp.where(seat == lane, means, 0.0), axis=0, keepdims=True)[:, 0:SEGS]
    for copy in results[:3]:
        copy.start()
    for copy in sent:
        copy.wait_send()
    for copy in results:
        copy.wait()


MESSAGES = 128
MOST = (0, 4, 1, 2, 5, 6)
FIRST = "SAB"
ORDER = [("S", 1), ("A", 1), ("B", 1), ("S", 2), ("Y", 1), ("n", 0), ("A", 2), ("B", 2), ("S", 3), ("n", 1), ("K",), ("F", 1),
    ("o",), ("Y", 2), ("A", 3), ("B", 3), ("S", 4), ("C", (1,), (0, 4)), ("F", 2), ("Y", 3), ("C", (2,), (0, 4)), ("r",), ("A", 4), ("B", 4), ("C", (1,), (1, 2)), ("Y", 4), ("m",), ("C", (1,), (5, 6)), ("C", (2,), (1, 2, 5, 6)), ("M",), ("f", 0), ("F", 3), ("C", (3,), MOST), ("w",), ("f", 1), ("C", (3, 2, 1), (3,)), ("F", 4), ("C", (0,), MOST), ("C", (0,), (3,)), ("l",), ("L", 0), ("L", 3), ("L", 2), ("L", 1),
]


def local(
    final_hidden, norm_gain, head_weight, token_ids, group_lengths, segment_ids, continues,
    layer_input, key_weight, key_gain, positions, key_rows,
):
    steps = np.arange(HD // 2, dtype=np.float64)
    freqs = np.exp(-(2.0 * steps / HD) * np.log(ROPE_BASE)).astype(np.float32)
    freqs = jnp.asarray(np.concatenate([freqs, freqs])[None, :])
    anywhere = pl.BlockSpec(memory_space=pl.ANY)
    smem = pl.BlockSpec(memory_space=pltpu.SMEM)
    f32, bf16 = jnp.float32, jnp.bfloat16
    logprob, entropy, mean, keys = pl.pallas_call(
        kernel,
        out_shape=(
            jax.ShapeDtypeStruct((2, ROWS), f32),
            jax.ShapeDtypeStruct((2, ROWS), f32),
            jax.ShapeDtypeStruct((1, SEGS), f32),
            jax.ShapeDtypeStruct((KROWS, BOTH), bf16),
        ),
        in_specs=[anywhere] * 10 + [smem] * 3,
        out_specs=(anywhere,) * 4,
        scratch_shapes=[
            pltpu.VMEM((DIM // HD, HD), f32),
            pltpu.VMEM((64, ROWS), jnp.int32),
            pltpu.VMEM((2, ROWS), jnp.int32),
            pltpu.VMEM((2, HD), f32),
            pltpu.VMEM((2, ROWS), jnp.int32),
            pltpu.VMEM((1, HD), f32),
            pltpu.VMEM((2, ROWS), f32),
            pltpu.VMEM((2, ROWS), f32),
            pltpu.VMEM((1, SEGS), f32),
            pltpu.VMEM((KROWS, BOTH), bf16),
            pltpu.VMEM((ROWS, DIM), bf16),
            pltpu.VMEM((8, DIM, ROWS), bf16),
            pltpu.VMEM((8, WROWS, DIM), bf16),
            pltpu.VMEM((2 * ROWS, DIM), bf16),
            pltpu.VMEM((DIM, BOTH), bf16),
            pltpu.VMEM((4, 1, BOTH), jnp.int32),
            pltpu.VMEM((4, 8, BOTH), f32),
            pltpu.VMEM((8, 8, ROWS), f32),
            pltpu.VMEM((8, ROWS), f32),
            pltpu.VMEM((16, 8, ROWS), f32),
            pltpu.VMEM((KPAD, HD), f32),
            pltpu.VMEM((8, KPAD, HD), f32),
            pltpu.VMEM((2, ROWS), jnp.int32),
            pltpu.SemaphoreType.DMA((14,)),
            pltpu.SemaphoreType.DMA((MESSAGES,)),
            pltpu.SemaphoreType.DMA((MESSAGES,)),
        ],
        compiler_params=pltpu.CompilerParams(
            collective_id=0, has_side_effects=True, vmem_limit_bytes=62 * 2**20
        ),
    )(
        final_hidden, head_weight, layer_input, key_weight,
        norm_gain.reshape(DIM // HD, HD), token_ids.reshape(-1, ROWS), segment_ids.reshape(2, ROWS),
        key_gain.reshape(2, HD), positions.reshape(2, ROWS), freqs, group_lengths, continues, key_rows,
    )
    outs = (logprob, entropy, mean, keys)

    def finish(*refs):
        copies = [pltpu.make_async_copy(refs[i], refs[4 + i], refs[8].at[i]) for i in range(4)]
        for copy in copies:
            copy.start()
        for copy in copies:
            copy.wait()

    logprob, entropy, mean, keys = pl.pallas_call(
        finish,
        out_shape=tuple(jax.ShapeDtypeStruct(a.shape, a.dtype) for a in outs),
        in_specs=[anywhere] * 4,
        out_specs=(anywhere,) * 4,
        scratch_shapes=[pltpu.SemaphoreType.DMA((4,))],
    )(*outs)
    return (logprob.reshape(-1), entropy.reshape(-1), mean.reshape(-1), keys)


def solution(mesh):
    in_specs = (
        P("grp", None),
        P(),
        P(("vocab", "grp"), None),
        P(),
        P(),
        P("grp"),
        P(),
        P("grp", None),
        P(None, "vocab"),
        P("vocab"),
        P("grp"),
        P("grp"),
    )
    out_specs = (P("grp"), P("grp"), P("grp"), P("grp", "vocab"))
    return jax.shard_map(local, mesh=mesh, in_specs=in_specs, out_specs=out_specs, check_vma=False)
```

```python
import jax
import jax.numpy as jnp
import numpy as np
from jax import lax
from jax.experimental import pallas as pl
from jax.experimental.pallas import tpu as pltpu
from jax.sharding import PartitionSpec as P

HD = 128
SEGS = 4
NORM_EPS = 1e-06
ROPE_BASE = 500000.0

NX, NY, NZ = 4, 4, 8
ROWS = 128
BOTH = 256
DIM = 2048
WROWS = 196
WPIECE = DIM // 4
SHARE = 352
ALONE = DIM - SHARE * NY
KROWS = 25
KPAD = 32
MESH = pl.DeviceIdType.MESH

TWO_PI_1 = 6.28125
TWO_PI_2 = float(np.float32(round((2 * np.pi - TWO_PI_1) * 2**20) / 2**20))
TWO_PI_3 = float(2 * np.pi - TWO_PI_1 - TWO_PI_2)


def place_of(d):
    return (0, 4, 1, 7, 2, 6, 3, 5).index(d)


def merged(maxes, sums, moments, picks):
    top = jnp.max(maxes, axis=0, keepdims=True)
    scale = jnp.exp(maxes - top)
    return (
        top,
        jnp.sum(sums * scale, axis=0, keepdims=True),
        jnp.sum(moments * scale, axis=0, keepdims=True),
        jnp.sum(picks, axis=0, keepdims=True),
    )


def kernel(
    hidden, weight, layer_input, key_weight,
    gain_in, tokens_in, segments_in, key_gain_in, positions_in, freqs_in, lengths, continues, key_rows,
    logprob_to, entropy_to, mean_to, keys_to,
    gain, tokens, segments, key_gain, positions, freqs, logprob_out, entropy_out, mean_out, keys_out,
    raw, held, wts, lin, kwt, toks, acc, gathered, part, parts,
    squares, all_squares, partner_segments,
    local_sems, send_sems, recv_sems,
):
    grp = lax.axis_index("grp")
    voc = lax.axis_index("vocab")
    x, z = lax.rem(grp, NX), lax.div(grp, NX)
    y, c = lax.div(voc, 2), lax.rem(voc, 2)

    def device(xx, yy, zz, cc):
        return (zz * NX + xx, yy * 2 + cc)

    def up(d):
        return device(x, y, lax.rem(z + d, NZ), c)

    x_up = device(lax.rem(x + 1, NX), y, z, c)
    x_down = device(lax.rem(x + NX - 1, NX), y, z, c)
    y_up = device(x, lax.rem(y + 1, NY), z, c)
    y_down = device(x, lax.rem(y + NY - 1, NY), z, c)
    sibling = device(x, y, z, 1 - c)
    partner = grp + 1 - 2 * lax.rem(x, 2)
    voc_peers = [(grp, lax.rem(voc + d, 8)) for d in range(1, 8)]

    ids = {}

    def remote(name, src, dst, to):
        number = ids.setdefault(name, len(ids))
        return pltpu.make_async_remote_copy(
            src_ref=src, dst_ref=dst, send_sem=send_sems.at[number], recv_sem=recv_sems.at[number],
            device_id=to, device_id_type=MESH,
        )

    sent = []

    def send(name, src, dst, to):
        copy = remote(name, src, dst, to)
        copy.start()
        sent.append(copy)

    def receive(name, dst, to):
        remote(name, dst, dst, to).wait_recv()

    local_copies = [
        pltpu.make_async_copy(hidden.at[pl.ds(pl.multiple_of(c * ROWS, ROWS), ROWS)], raw, local_sems.at[0]),
        pltpu.make_async_copy(weight, wts.at[0], local_sems.at[1]),
        pltpu.make_async_copy(layer_input, lin, local_sems.at[2]),
        pltpu.make_async_copy(key_weight, kwt, local_sems.at[3]),
    ]
    small = [
        pltpu.make_async_copy(src, dst, local_sems.at[4 + i]) for i, (src, dst) in enumerate((
            (gain_in, gain), (tokens_in, tokens), (segments_in, segments),
            (key_gain_in, key_gain), (positions_in, positions), (freqs_in, freqs),
        ))
    ]
    results = [
        pltpu.make_async_copy(src, dst, local_sems.at[10 + i]) for i, (src, dst) in enumerate((
            (logprob_out, logprob_to), (entropy_out, entropy_to), (mean_out, mean_to), (keys_out, keys_to),
        ))
    ]

    barrier = pltpu.get_barrier_semaphore()
    partners = [(partner, lax.rem(voc + d, 8)) for d in range(8)]
    other_x = device(lax.rem(x + 3 + 2 * lax.rem(x, 2), NX), y, z, c)
    peers = [other_x] + partners + [up(d) for d in (1, 7, 2, 6, 3, 5, 4)] + voc_peers
    for peer in peers:
        pl.semaphore_signal(barrier, inc=1, device_id=peer, device_id_type=MESH)
    for copy in local_copies[:1] + small + local_copies[1:]:
        copy.start()
    pl.semaphore_wait(barrier, len(peers))

    def piece(q):
        return pl.ds(q * WPIECE, WPIECE)

    def own_piece(way, first, count):
        cols = pl.ds(first * WPIECE, count * WPIECE)
        slot, to = (1, x_up) if way == "+" else (2, x_down)
        send(f"w{way}{first}", weight.at[:, cols], wts.at[slot, :, cols], to)

    own_piece("+", 0, 1)
    own_piece("-", 2, 1)

    def to_sibling(slot, first, count):
        cols = pl.ds(first * WPIECE, count * WPIECE)
        send(f"s{slot}{first}", wts.at[slot, :, cols], wts.at[4 + slot, :, cols], sibling)

    def from_sibling(slot, first, count):
        cols = pl.ds(first * WPIECE, count * WPIECE)
        receive(f"s{slot}{first}", wts.at[4 + slot, :, cols], sibling)

    def weights_near(i):
        receive(f"w+{i}", wts.at[1, :, piece(i)], x_up)
        send(f"wf+{i}", wts.at[1, :, piece(i)], wts.at[3, :, piece(i)], x_up)
        receive(f"w-{i + 2}", wts.at[2, :, piece(i + 2)], x_down)
        send(f"wf-{i + 2}", wts.at[2, :, piece(i + 2)], wts.at[3, :, piece(i + 2)], x_down)
        if i == 1:
            to_sibling(1, 0, 2)
            to_sibling(2, 2, 2)

    def weights_rest():
        cols = pl.ds(2 * WPIECE, 2 * WPIECE)
        receive("w+2", wts.at[1, :, cols], x_up)
        to_sibling(1, 2, 2)
        cols = pl.ds(0, 2 * WPIECE)
        receive("w-0", wts.at[2, :, cols], x_down)
        to_sibling(2, 0, 2)

    def weights_far(i):
        receive(f"wf+{i}", wts.at[3, :, piece(i)], x_up)
        to_sibling(3, i, 1)
        receive(f"wf-{i + 2}", wts.at[3, :, piece(i + 2)], x_down)
        to_sibling(3, i + 2, 1)

    local_copies[0].wait()
    small[0].wait()
    total = jnp.zeros((ROWS, HD), jnp.float32)
    for j in range(DIM // HD):
        block = raw[:, j * HD:(j + 1) * HD].astype(jnp.float32)
        total = total + block * block
    inverse = lax.rsqrt(jnp.sum(total, axis=1, keepdims=True) / DIM + NORM_EPS)
    for j in range(DIM // HD):
        block = raw[:, j * HD:(j + 1) * HD].astype(jnp.float32)
        held[0, j * HD:(j + 1) * HD, :] = (block * inverse * gain[j:j + 1, :]).T.astype(jnp.bfloat16)

    def features(d, first, count):
        return held.at[place_of(d), pl.ds(first, count), :]

    def share(yy, first=0):
        return pl.multiple_of(ALONE + SHARE * lax.rem(yy, NY) + first, 16)

    LAST = {"S+": 3, "S-": 4, "A+": 4, "A-": 3, "B+": 4, "B-": 3}

    def away(way, k):
        return (NZ - k) % NZ if way == "+" else k

    def z_part(kind, d):
        if kind == "S":
            return features(d, share(y), SHARE)
        return features(d, 0 if kind == "A" else ALONE // 2, ALONE // 2)

    def z_send(kind, way, k):
        send(
            f"z{kind}{way}{k}", z_part(kind, away(way, k - 1)), z_part(kind, away(way, k)),
            up(1) if way == "+" else up(NZ - 1),
        )

    def z_receive(kind, k):
        for way in "+-":
            if k > LAST[kind + way]:
                continue
            d = away(way, k)
            receive(f"z{kind}{way}{k}", z_part(kind, d), up(1))
            if k < LAST[kind + way]:
                z_send(kind, way, k + 1)
        if kind == "S":
            ref = shares(k, share(y), SHARE)
            send(f"y+{k}", ref, ref, y_up)
            send(f"y-{k}", ref, ref, y_down)

    def shares(k, first, count):
        slots = pl.ds(2 * k, 2) if k < 4 else pl.ds(1, 1)
        return held.at[slots, pl.ds(first, count), :]

    half_share = SHARE // 2

    def y_receive(k):
        below, above = y + NY - 1, y + 1
        receive(f"y+{k}", shares(k, share(below), SHARE), y_up)
        ref = shares(k, share(below), half_share)
        send(f"yf+{k}", ref, ref, y_up)
        receive(f"y-{k}", shares(k, share(above), SHARE), y_down)
        ref = shares(k, share(above, half_share), half_share)
        send(f"yf-{k}", ref, ref, y_down)

    def y_finish(k):
        receive(f"yf+{k}", shares(k, share(y + 2), half_share), y_up)
        receive(f"yf-{k}", shares(k, share(y + 2, half_share), half_share), y_down)

    def z_start(kinds):
        for kind in kinds:
            for way in "+-":
                z_send(kind, way, 1)

    z_start(FIRST)
    own_piece("+", 1, 1)
    own_piece("-", 3, 1)
    own_piece("+", 2, 2)
    own_piece("-", 0, 2)
    send("w0", weight, wts.at[4], sibling)
    for copy in small[1:]:
        copy.wait()
    send("g", segments, partner_segments, partners[0])

    row_ids = lax.broadcasted_iota(jnp.int32, (KPAD, BOTH), 0)
    col_ids = lax.broadcasted_iota(jnp.int32, (KPAD, BOTH), 1)
    wanted = jnp.zeros((KPAD, BOTH), jnp.int32)
    for i in range(KROWS):
        wanted = jnp.where(row_ids == i, key_rows[i], wanted)
    picks = jnp.where(col_ids == wanted, 1.0, 0.0)
    local_copies[2].wait()
    local_copies[3].wait()
    chosen = jnp.dot(picks.astype(jnp.bfloat16), lin[...], preferred_element_type=jnp.float32)
    projected = jnp.dot(chosen.astype(jnp.bfloat16), kwt[...], preferred_element_type=jnp.float32)
    squares[...] = jnp.broadcast_to(jnp.sum(projected * projected, axis=1, keepdims=True), (KPAD, HD))
    for i, peer in enumerate(voc_peers):
        send(f"k{i + 1}", squares, all_squares.at[i + 1], peer)

    for p in range(4):
        acc[p, 0:1, :] = jnp.full((1, BOTH), -jnp.inf, jnp.float32)
        acc[p, 1:8, :] = jnp.zeros((7, BOTH), jnp.float32)
        for half, d in enumerate((0, 4, 1, 7, 2, 6, 3, 5)[2 * p:2 * p + 2]):
            row = (lax.rem(z + d, NZ) * NX + x) * 2 + c
            toks[p, 0:1, half * ROWS:(half + 1) * ROWS] = tokens[pl.ds(row, 1), :]

    def chunk(p, w):
        other, turn = divmod(w, 4)
        shift = (0, NX - 1, 1, 2)[turn]
        first = (y * 2 + lax.rem(c + other, 2)) * (WROWS * NX * NZ) + (z * NX + lax.rem(x + shift, NX)) * WROWS
        logits = lax.dot_general(
            wts[w], jnp.concatenate([held[2 * p], held[2 * p + 1]], axis=1),
            (((1,), (0,)), ((), ())), preferred_element_type=jnp.float32
        ).astype(jnp.bfloat16).astype(jnp.float32)
        old = acc[p, 0:1, :]
        top = jnp.maximum(old, jnp.max(logits, axis=0, keepdims=True))
        shifted = jnp.exp(logits - top)
        scale = jnp.exp(old - top)
        hit = lax.broadcasted_iota(jnp.int32, (WROWS, BOTH), 0) == toks[p, 0:1, :] - first
        acc[p, 0:1, :] = top
        acc[p, 1:2, :] = acc[p, 1:2, :] * scale + jnp.sum(shifted, axis=0, keepdims=True)
        acc[p, 2:3, :] = acc[p, 2:3, :] * scale + jnp.sum(shifted * logits, axis=0, keepdims=True)
        acc[p, 3:4, :] = acc[p, 3:4, :] + jnp.sum(jnp.where(hit, logits, 0.0), axis=0, keepdims=True)

    def run(pairs, slots):
        for p in pairs:
            for w in slots:
                chunk(p, w)

    def give(p):
        for half, d in enumerate((0, 4, 1, 7, 2, 6, 3, 5)[2 * p:2 * p + 2]):
            if d:
                send(f"a{d}", acc.at[p, :, pl.ds(half * ROWS, ROWS)], gathered.at[NZ - d], up(d))

    def finish_keys():
        for i in range(7):
            receive(f"k{i + 1}", all_squares.at[i + 1], sibling)
        square_sum = squares[...]
        for i in range(7):
            square_sum = square_sum + all_squares[i + 1]
        spread = jnp.sqrt(square_sum / (HD * 16) + NORM_EPS)
        places_row = jnp.concatenate([positions[0:1, :], positions[1:2, :]], axis=1).astype(jnp.float32)
        places = jnp.sum(picks * places_row, axis=1, keepdims=True)
        angles = places * freqs[0:1, :]
        turns = jnp.floor(angles * (0.5 / np.pi) + 0.5)
        angles = ((angles - turns * TWO_PI_1) - turns * TWO_PI_2) - turns * TWO_PI_3
        lanes = lax.broadcasted_iota(jnp.int32, (KPAD, HD), 1)
        cosine = jnp.cos(angles)
        sine = jnp.sin(angles)
        sine = jnp.where(lanes < HD // 2, -sine, sine)
        for head in range(2):
            values = projected[:, head * HD:(head + 1) * HD] / spread * key_gain[head:head + 1, :]
            turned = values * cosine + pltpu.roll(values, HD // 2, 1) * sine
            keys_out[:, head * HD:(head + 1) * HD] = turned[0:KROWS].astype(jnp.bfloat16)

        results[3].start()

    def start_chunks():
        local_copies[1].wait()
        receive("w0", wts.at[4], sibling)

    def near_from_sibling():
        for first in (0, 2):
            from_sibling(1, first, 2)
            from_sibling(2, first, 2)

    def far_from_sibling():
        for q in (0, 2, 1, 3):
            from_sibling(3, q, 1)

    def last_chunk(p):
        chunk(p, 7)
        give(p)

    marks = []

    def settle():
        for copy in sent[:marks[0]]:
            copy.wait_send()
        del sent[:marks[0]]

    events = {
        "M": lambda: marks.append(len(sent)), "w": settle,
        "S": lambda k: z_receive("S", k), "A": lambda k: z_receive("A", k),
        "B": lambda k: z_receive("B", k), "a": z_start,
        "Y": y_receive, "F": y_finish, "K": finish_keys,
        "n": weights_near, "r": weights_rest, "f": weights_far,
        "o": start_chunks, "m": near_from_sibling, "l": far_from_sibling,
        "C": run, "L": last_chunk,
    }
    for name, *rest in ORDER:
        events[name](*rest)

    gathered[0] = acc[0, :, 0:ROWS]
    for d in range(1, NZ):
        receive(f"a{d}", gathered.at[NZ - d], up(d))
    stats = merged(*(gathered[:, i, :] for i in range(4)))
    for i in range(4):
        part[i:i + 1, :] = stats[i]
    part[4:8, :] = jnp.zeros((4, ROWS), jnp.float32)
    mine = c * NY + y
    for d in (4, 3, 5, 2, 6, 0, 1, 7):
        send(f"u{d}", part, parts.at[8 + mine], partners[d])
        if d:
            send(f"v{d}", part, parts.at[mine], voc_peers[d - 1])
    parts[mine] = part[...]

    def place(d):
        source = lax.rem(voc + 8 - d, 8)
        return lax.rem(source, 2) * NY + lax.div(source, 2)

    for d in range(1, 8):
        receive(f"v{d}", parts.at[place(d)], sibling)
    receive("g", partner_segments, sibling)
    for d in range(8):
        receive(f"u{d}", parts.at[8 + place(d)], sibling)

    lane = lax.broadcasted_iota(jnp.int32, (1, ROWS), 1)
    seat = lax.broadcasted_iota(jnp.int32, (8, ROWS), 0)
    totals = []
    for first, group, labels in ((0, grp, segments), (8, partner, partner_segments)):
        length = lengths[group]
        sums = jnp.zeros((8, ROWS), jnp.float32)
        counts = jnp.zeros((8, ROWS), jnp.float32)
        last = jnp.zeros((1, ROWS), jnp.float32)
        for half in range(2):
            start = first + half * NY
            top, expsum, moment, picked = merged(*(parts[start:start + NY, i, :] for i in range(4)))
            logsum = top + jnp.log(expsum)
            slot = lane + half * ROWS
            live = slot < length
            logprob = jnp.where(live, picked - logsum, 0.0)
            label = labels[half:half + 1, :]
            if first == 0:
                logprob_out[half:half + 1, :] = logprob
                entropy_out[half:half + 1, :] = jnp.where(live, logsum - moment / expsum, 0.0)
            last = last + jnp.where(slot == length - 1, label.astype(jnp.float32), 0.0)
            member = seat == jnp.where(live, label, SEGS)
            sums = sums + jnp.where(member, logprob, 0.0)
            counts = counts + jnp.where(member, 1.0, 0.0)
        if first == 0:
            for copy in results[:2]:
                copy.start()
        totals.append((
            jnp.sum(sums, axis=1, keepdims=True), jnp.sum(counts, axis=1, keepdims=True),
            jnp.sum(last, axis=1, keepdims=True),
        ))
    (sums, counts, last), (got_sums, got_counts, _) = totals
    row = lax.broadcasted_iota(jnp.int32, (8, 1), 0).astype(jnp.float32)
    even = lax.rem(x, 2) == 0
    joined = continues[grp - lax.rem(grp, 2)] == 1
    got_last = jnp.max(jnp.where((got_counts > 0) & (row < SEGS), row, 0.0), axis=0, keepdims=True)
    source = jnp.where(even, 0.0, got_last)
    target = jnp.where(even, last, 0.0)
    extra_sum = jnp.sum(jnp.where(row == source, got_sums, 0.0), axis=0, keepdims=True)
    extra_count = jnp.sum(jnp.where(row == source, got_counts, 0.0), axis=0, keepdims=True)
    update = joined & (row == target)
    total_sum = sums + jnp.where(update, extra_sum, 0.0)
    total_count = counts + jnp.where(update, extra_count, 0.0)
    means = total_sum / jnp.maximum(total_count, 1.0)
    mean_out[...] = jnp.sum(jnp.where(seat == lane, means, 0.0), axis=0, keepdims=True)[:, 0:SEGS]
    results[2].start()
    for copy in sent:
        copy.wait_send()
    for copy in results:
        copy.wait()


MESSAGES = 128
MOST = (0, 4, 1, 2, 5, 6)
FIRST = "SAB"
ORDER = [("S", 1), ("A", 1), ("B", 1), ("S", 2), ("Y", 1), ("n", 0), ("A", 2), ("B", 2), ("S", 3), ("n", 1), ("K",), ("F", 1),
    ("o",), ("Y", 2), ("A", 3), ("B", 3), ("S", 4), ("C", (1,), (0, 4)), ("F", 2), ("Y", 3), ("C", (2,), (0, 4)), ("r",), ("A", 4), ("B", 4), ("C", (1,), (1, 2)), ("Y", 4), ("m",), ("C", (1,), (5, 6)), ("C", (2,), (1, 2, 5, 6)), ("M",), ("f", 0), ("F", 3), ("C", (3,), MOST), ("w",), ("f", 1), ("C", (3, 2, 1), (3,)), ("F", 4), ("C", (0,), MOST), ("C", (0,), (3,)), ("l",), ("L", 0), ("L", 3), ("L", 2), ("L", 1),
]


def local(
    final_hidden, norm_gain, head_weight, token_ids, group_lengths, segment_ids, continues,
    layer_input, key_weight, key_gain, positions, key_rows,
):
    steps = np.arange(HD // 2, dtype=np.float64)
    freqs = np.exp(-(2.0 * steps / HD) * np.log(ROPE_BASE)).astype(np.float32)
    freqs = jnp.asarray(np.concatenate([freqs, freqs])[None, :])
    anywhere = pl.BlockSpec(memory_space=pl.ANY)
    smem = pl.BlockSpec(memory_space=pltpu.SMEM)
    f32, bf16 = jnp.float32, jnp.bfloat16
    logprob, entropy, mean, keys = pl.pallas_call(
        kernel,
        out_shape=(
            jax.ShapeDtypeStruct((2, ROWS), f32),
            jax.ShapeDtypeStruct((2, ROWS), f32),
            jax.ShapeDtypeStruct((1, SEGS), f32),
            jax.ShapeDtypeStruct((KROWS, BOTH), bf16),
        ),
        in_specs=[anywhere] * 10 + [smem] * 3,
        out_specs=(anywhere,) * 4,
        scratch_shapes=[
            pltpu.VMEM((DIM // HD, HD), f32),
            pltpu.VMEM((64, ROWS), jnp.int32),
            pltpu.VMEM((2, ROWS), jnp.int32),
            pltpu.VMEM((2, HD), f32),
            pltpu.VMEM((2, ROWS), jnp.int32),
            pltpu.VMEM((1, HD), f32),
            pltpu.VMEM((2, ROWS), f32),
            pltpu.VMEM((2, ROWS), f32),
            pltpu.VMEM((1, SEGS), f32),
            pltpu.VMEM((KROWS, BOTH), bf16),
            pltpu.VMEM((ROWS, DIM), bf16),
            pltpu.VMEM((8, DIM, ROWS), bf16),
            pltpu.VMEM((8, WROWS, DIM), bf16),
            pltpu.VMEM((2 * ROWS, DIM), bf16),
            pltpu.VMEM((DIM, BOTH), bf16),
            pltpu.VMEM((4, 1, BOTH), jnp.int32),
            pltpu.VMEM((4, 8, BOTH), f32),
            pltpu.VMEM((8, 8, ROWS), f32),
            pltpu.VMEM((8, ROWS), f32),
            pltpu.VMEM((16, 8, ROWS), f32),
            pltpu.VMEM((KPAD, HD), f32),
            pltpu.VMEM((8, KPAD, HD), f32),
            pltpu.VMEM((2, ROWS), jnp.int32),
            pltpu.SemaphoreType.DMA((14,)),
            pltpu.SemaphoreType.DMA((MESSAGES,)),
            pltpu.SemaphoreType.DMA((MESSAGES,)),
        ],
        compiler_params=pltpu.CompilerParams(
            collective_id=0, has_side_effects=True, vmem_limit_bytes=62 * 2**20
        ),
    )(
        final_hidden, head_weight, layer_input, key_weight,
        norm_gain.reshape(DIM // HD, HD), token_ids.reshape(-1, ROWS), segment_ids.reshape(2, ROWS),
        key_gain.reshape(2, HD), positions.reshape(2, ROWS), freqs, group_lengths, continues, key_rows,
    )
    outs = (logprob, entropy, mean, keys)

    def finish(*refs):
        copies = [pltpu.make_async_copy(refs[i], refs[4 + i], refs[8].at[i]) for i in range(4)]
        for copy in copies:
            copy.start()
        for copy in copies:
            copy.wait()

    logprob, entropy, mean, keys = pl.pallas_call(
        finish,
        out_shape=tuple(jax.ShapeDtypeStruct(a.shape, a.dtype) for a in outs),
        in_specs=[anywhere] * 4,
        out_specs=(anywhere,) * 4,
        scratch_shapes=[pltpu.SemaphoreType.DMA((4,))],
    )(*outs)
    return (logprob.reshape(-1), entropy.reshape(-1), mean.reshape(-1), keys)


def solution(mesh):
    in_specs = (
        P("grp", None),
        P(),
        P(("vocab", "grp"), None),
        P(),
        P(),
        P("grp"),
        P(),
        P("grp", None),
        P(None, "vocab"),
        P("vocab"),
        P("grp"),
        P("grp"),
    )
    out_specs = (P("grp"), P("grp"), P("grp"), P("grp", "vocab"))
    return jax.shard_map(local, mesh=mesh, in_specs=in_specs, out_specs=out_specs, check_vma=False)
```
